128 devices in a mesh: flow: 32 (over z, y, core), trans: 4 (over x).
Axes of the slice: x: 4, y: 4, z: 4, core: 2. Of those that a mesh axis runs over, the one named last changes fastest.
Arguments:
- concentration: float32 [4, 512, 64, 256], P(None, 'flow', 'trans'), may hold values from 0 to 2
- stratum: int32 [512, 64, 256], P('flow', 'trans'), may hold values from 0 to 15
- porosity: float32 [16], replicated, may hold values from 0.1 to 0.4
- dispersion_table: float32 [16, 2], replicated, may hold values from 512 to 15360
- transverse_table: float32 [16], replicated, may hold values from 0.2 to 2
- exchange_table: float32 [16], replicated, may hold values from 0.01 to 0.2
- decay_table: float32 [16], replicated, may hold values from 0.01 to 0.2
Outputs:
- new_concentration: float32 [4, 512, 64, 256], P(None, 'flow', 'trans')
The draws below stay inside these ranges and needn't reach their ends.
All inputs are finite; a program needn't handle non-finite values.
Results may differ from the reference program's by a relative error of at most 0.001.
Values sent between devices are 32-bit elements; how exact they have to be, the bound alone decides.
A program may use at most 128 MiB of HBM per device.

```python
import math
import jax
import jax.numpy as jnp
from jax import lax

NZ = 256
STRATA = 16
NX = 512
NY = 64


def draw_concentration(key, part):
    rough_key = jax.random.fold_in(key, 11)
    phase_key = jax.random.fold_in(key, 23)
    rough = jax.random.uniform(rough_key, (4, NX, NY, NZ), jnp.float32)
    phase = jax.random.uniform(phase_key, (4, 1, 1, 1), jnp.float32)
    along = (jnp.arange(NX, dtype=jnp.float32)[None, :, None, None] + 0.5) / NX
    smooth = 0.9 + 0.4 * jnp.sin(2.0 * math.pi * (along + phase))
    values = smooth + (rough - 0.5)
    return values.astype(jnp.float32)


def touch_ends(values, rng, low, top_value):
    index_at = [jax.random.randint(jax.random.fold_in(rng, axis), (), 0, length) for axis, length in enumerate(values.shape)]
    longest = values.shape.index(max(values.shape))
    neighbour = index_at[:longest] + [(index_at[longest] + 1) % values.shape[longest]] + index_at[longest + 1:]
    return values.at[tuple(index_at)].set(low).at[tuple(neighbour)].set(top_value)


def setup_inputs(seed: int = 0) -> dict:
    arg_keys = jax.random.split(jax.random.key(seed), 8)
    return {
        "concentration": draw_concentration(jax.random.fold_in(arg_keys[7], 71), 0),
        "stratum": touch_ends(jax.random.randint(arg_keys[1], (NX, NY, NZ), 0, STRATA), jax.random.fold_in(arg_keys[1], 1), 0, STRATA - 1).astype(jnp.int32),
        "porosity": jnp.clip(jax.random.uniform(arg_keys[2], (STRATA,), jnp.float32, 0.1, 0.4), 0.1, 0.4),
        "dispersion_table": jnp.clip(jnp.exp(jax.random.uniform(arg_keys[3], (STRATA, 2), jnp.float32, math.log(512.0), math.log(15360.0))), 512.0, 15360.0),
        "transverse_table": jnp.clip(jnp.exp(jax.random.uniform(arg_keys[4], (STRATA,), jnp.float32, math.log(0.2), math.log(2.0))), 0.2, 2.0),
        "exchange_table": jnp.clip(jnp.exp(jax.random.uniform(arg_keys[5], (STRATA,), jnp.float32, math.log(0.01), math.log(0.2))), 0.01, 0.2),
        "decay_table": jnp.clip(jnp.exp(jax.random.uniform(arg_keys[6], (STRATA,), jnp.float32, math.log(0.01), math.log(0.2))), 0.01, 0.2),
    }


def harmonic(first, second):
    return 2.0 * first * second / (first + second)

def assemble(diagonal, exchange, decay):
    nothing = jnp.zeros_like(exchange)
    block_rows = [[diagonal[0] + exchange + decay, nothing, -exchange, nothing], [-decay, diagonal[1] + exchange, nothing, -exchange], [-exchange, nothing, diagonal[2] + exchange + decay, nothing], [nothing, -exchange, -decay, diagonal[3] + exchange]]
    return jnp.stack([jnp.stack(entries) for entries in block_rows])

def cells_last(field):
    return jnp.moveaxis(field, 0, -1)

def line_solve(diagonal, exchange, decay, left_face, right_face, source):
    unit_block = jnp.eye(4, dtype=diagonal.dtype)
    line_count = diagonal.shape[1]

    def forward(state_pair, inputs_cell):
        upper_prev, vector_prev = state_pair
        diagonal_cell, exchange_cell, decay_cell, left_num, right_num, forcing = inputs_cell
        cell_block = jnp.moveaxis(assemble(jnp.transpose(diagonal_cell), exchange_cell, decay_cell), -1, 0)
        pivot_block = cell_block + left_num[:, :, None] * upper_prev
        columns = jnp.concatenate([-(right_num[:, None, :] * unit_block), (forcing + left_num * vector_prev)[:, :, None]], axis=2)
        solved = jnp.linalg.solve(pivot_block, columns)
        upper_part = solved[:, :, :4]
        vector_part = solved[:, :, 4]
        return ((upper_part, vector_part), (upper_part, vector_part))
    start_pair = (jnp.zeros((line_count, 4, 4), diagonal.dtype), jnp.zeros((line_count, 4), diagonal.dtype))
    ignored, stored = lax.scan(forward, start_pair, (diagonal, exchange, decay, left_face, right_face, source))

    def backward(following, inputs_cell):
        upper_part, vector_part = inputs_cell
        current = vector_part - jnp.einsum('bmn,bn->bm', upper_part, following)
        return (current, current)
    final_state, result = lax.scan(backward, jnp.zeros((line_count, 4), diagonal.dtype), stored, reverse=True)
    return result

def reference(concentration, stratum, porosity, dispersion_table, transverse_table, exchange_table, decay_table):
    transverse = transverse_table[stratum]
    padded_mobile = jnp.pad(concentration[:2], ((0, 0), (0, 0), (1, 1), (1, 1)))
    padded_trans = jnp.pad(transverse, ((0, 0), (1, 1), (1, 1)))

    def plane_solve(row_index):
        strata_row = lax.dynamic_index_in_dim(stratum, row_index, 1, keepdims=False)
        conc_row = lax.dynamic_index_in_dim(concentration, row_index, 2, keepdims=False)
        mobile_window = lax.dynamic_slice_in_dim(padded_mobile, row_index, 3, 2)
        trans_window = lax.dynamic_slice_in_dim(padded_trans, row_index, 3, 1)
        centre_num = trans_window[:, 1, 1:NZ + 1]
        centre_conc = mobile_window[:, :, 1, 1:NZ + 1]
        flux = jnp.zeros_like(centre_conc)
        for offset_y, offset_z in ((2, 1), (0, 1), (1, 2), (1, 0)):
            neighbour_num = trans_window[:, offset_y, offset_z:offset_z + NZ]
            neighbour_conc = mobile_window[:, :, offset_y, offset_z:offset_z + NZ]
            flux = flux + harmonic(centre_num, neighbour_num) * (neighbour_conc - centre_conc)
        porosity_cell = porosity[strata_row]
        dispersion = jnp.moveaxis(dispersion_table[strata_row], -1, 0)
        exchange = exchange_table[strata_row]
        decay = decay_table[strata_row]
        padded_flow = jnp.pad(dispersion, ((0, 0), (1, 1), (0, 0)))
        right_mobile = harmonic(dispersion, padded_flow[:, 2:])
        left_mobile = harmonic(dispersion, padded_flow[:, :-2])
        zero_faces = jnp.zeros_like(left_mobile)
        left_face = jnp.concatenate([left_mobile, zero_faces])
        right_face = jnp.concatenate([right_mobile, zero_faces])
        capacity = jnp.stack([porosity_cell, porosity_cell, 1.0 - porosity_cell, 1.0 - porosity_cell])
        source = capacity * conc_row + jnp.concatenate([flux, jnp.zeros_like(flux)])
        diagonal = capacity + jnp.concatenate([left_mobile + right_mobile, zero_faces])
        return line_solve(cells_last(diagonal), exchange, decay, cells_last(left_face), cells_last(right_face), cells_last(source))
    solved = lax.map(plane_solve, jnp.arange(NY, dtype=jnp.int32))
    return jnp.transpose(solved, (3, 1, 0, 2))
```

```python
import functools

import jax
import jax.numpy as jnp
from jax import lax
from jax.experimental import pallas as pl
from jax.experimental.pallas import tpu as pltpu
from jax.sharding import PartitionSpec as P

MESH = pl.DeviceIdType.MESH
STRATA = 16
CELLS = 16
PLANES = 16
LANES = 128
HALVES = 2
ROWS = HALVES * PLANES
SLOT = 16
BACK = 8
TABLES = (
    "u_a",
    "u_b",
    "u_t",
    "g_a",
    "g_b",
    "eta",
    "por",
    "src_a",
    "src_b",
    "src_ab",
    "im_a",
    "ex_a",
    "im_b",
    "ex_b",
    "im_ab",
    "ex_ab",
)
FIELDS = (
    "w_a",
    "q_a",
    "r_a",
    "w_b",
    "q_b",
    "r_b",
    "q_cum_a",
    "w_cum_a",
    "q_cum_b",
    "w_cum_b",
    "eta",
    "s_a",
    "s_b",
    "v_a",
    "v_b",
    "v_l",
    "v_r",
    "p_b",
    "y_l",
    "y_r",
    "im_a",
    "ex_a",
    "im_b",
    "ex_b",
    "ex_ab",
)


def kernel(
    flow_size,
    trans_size,
    conc_hbm,
    strat_hbm,
    por_hbm,
    disp_hbm,
    trans_hbm,
    exch_hbm,
    decay_hbm,
    out_ref,
    por_ref,
    disp_ref,
    trans_ref,
    exch_ref,
    decay_ref,
    conc,
    strat,
    tables,
    fields,
    edges,
    halo,
    send,
    recv,
    back,
    got,
    load_sem,
    edge_send_sem,
    edge_recv_sem,
    out_send_sem,
    out_recv_sem,
    back_send_sem,
    back_recv_sem,
):
    f32 = jnp.float32
    me = lax.axis_index("flow")
    group = lax.axis_index("trans")
    loads = []
    for half in range(HALVES):
        lanes = pl.ds(half * LANES, LANES)
        loads.append(
            pltpu.make_async_copy(strat_hbm.at[:, lanes], strat.at[half], load_sem.at[half])
        )
    for half in range(HALVES):
        lanes = pl.ds(half * LANES, LANES)
        loads.append(
            pltpu.make_async_copy(
                conc_hbm.at[:, lanes], conc.at[half], load_sem.at[HALVES + half]
            )
        )
    table_loads = [
        pltpu.make_async_copy(src, dst, load_sem.at[2 * HALVES + index])
        for index, (src, dst) in enumerate(
            (
                (por_hbm, por_ref),
                (disp_hbm, disp_ref),
                (trans_hbm, trans_ref),
                (exch_hbm, exch_ref),
                (decay_hbm, decay_ref),
            )
        )
    ]
    for copy in table_loads + loads:
        copy.start()

    barrier = pltpu.get_barrier_semaphore()

    def greet(step, carry):
        peer = lax.rem(me + step, flow_size)
        pl.semaphore_signal(barrier, inc=1, device_id={"flow": peer}, device_id_type=MESH)
        return carry

    for step in (1, trans_size - 1):
        pl.semaphore_signal(
            barrier,
            inc=1,
            device_id={"trans": lax.rem(group + step, trans_size)},
            device_id_type=MESH,
        )
    lax.fori_loop(1, flow_size, greet, 0)

    lane = lax.broadcasted_iota(jnp.int32, (8, LANES), 1)

    def lane_table(read):
        table = jnp.full((8, LANES), read(0), f32)
        for stratum in range(1, STRATA):
            table = jnp.where(lane == stratum, read(stratum), table)
        return table

    for copy in table_loads:
        copy.wait()
    por = lane_table(lambda k: por_ref[k])
    disp_a = lane_table(lambda k: disp_ref[0, k])
    disp_b = lane_table(lambda k: disp_ref[1, k])
    trans = lane_table(lambda k: trans_ref[k])
    exch = lane_table(lambda k: exch_ref[k])
    decay = lane_table(lambda k: decay_ref[k])
    rest = 1.0 - por
    m_a = 1.0 / (rest + exch + decay)
    m_b = 1.0 / (rest + exch)
    values = {
        "u_a": 0.5 / disp_a,
        "u_b": 0.5 / disp_b,
        "u_t": 0.5 / trans,
        "g_a": por + decay + exch * (rest + decay) * m_a,
        "g_b": por + exch * rest * m_b,
        "eta": decay + exch * exch * decay * m_a * m_b,
        "por": por,
        "src_a": exch * rest * m_a,
        "src_b": exch * rest * m_b,
        "src_ab": exch * m_b * decay * rest * m_a,
        "im_a": rest * m_a,
        "ex_a": exch * m_a,
        "im_b": rest * m_b,
        "ex_b": exch * m_b,
        "im_ab": decay * m_b * rest * m_a,
        "ex_ab": decay * m_b * exch * m_a,
    }
    for index, name in enumerate(TABLES):
        tables[index] = values[name]

    def look(name, picked):
        table = tables[TABLES.index(name)]
        wide = jnp.concatenate([table] * (picked.shape[0] // 8), axis=0)
        return jnp.take_along_axis(wide, picked, axis=1, mode="promise_in_bounds")

    def spot(cell):
        start = cell * PLANES
        if not isinstance(cell, int):
            start = pl.multiple_of(start, PLANES)
        return pl.ds(start, PLANES)

    def strata_of(cell):
        return strat[:, spot(cell), :].reshape(ROWS, LANES)

    def conc_of(component, cell):
        return conc[:, spot(component * CELLS + cell), :].reshape(ROWS, LANES)

    def get(name, cell):
        return fields[FIELDS.index(name), :, spot(cell), :].reshape(ROWS, LANES)

    def put(name, cell, value):
        fields[FIELDS.index(name), :, spot(cell), :] = value.reshape(HALVES, PLANES, LANES)

    for copy in loads:
        copy.wait()

    for side, plane in ((0, 0), (1, PLANES - 1)):
        for half in range(HALVES):
            rows = pl.ds(plane, CELLS, stride=PLANES)
            picked = strat[half, rows, :]
            edges[side, half, pl.ds(0, CELLS), :] = look("u_t", picked)
            for component in range(2):
                rows = pl.ds(component * CELLS * PLANES + plane, CELLS, stride=PLANES)
                edges[side, half, pl.ds((component + 1) * CELLS, CELLS), :] = conc[half, rows, :]

    pl.semaphore_wait(barrier, flow_size + 1)

    def edge_copy(side):
        return pltpu.make_async_remote_copy(
            src_ref=edges.at[side],
            dst_ref=halo.at[1 - side],
            send_sem=edge_send_sem.at[side],
            recv_sem=edge_recv_sem.at[1 - side],
            device_id={"trans": group - 1 + 2 * side},
            device_id_type=MESH,
        )

    has_side = (group > 0, group < trans_size - 1)

    @pl.when(has_side[0])
    def _():
        edge_copy(0).start()

    @pl.when(has_side[1])
    def _():
        edge_copy(1).start()

    def eliminate(state, name, r, g_next):
        k, alpha, delta = state
        w = 1.0 / (1.0 + r * (k + delta))
        rw = r * w
        q = rw * k
        return (k * w, alpha + q * delta, g_next + delta * w), w, q, rw

    first = strata_of(0)
    zero = jnp.zeros((ROWS, LANES), f32)
    u_a0, u_b0 = look("u_a", first), look("u_b", first)
    start = (
        (1.0 / u_a0, zero, look("g_a", first)),
        (1.0 / u_b0, zero, look("g_b", first)),
        u_a0,
        u_b0,
    )

    def forward(cell, state, last=False):
        state_a, state_b, u_a, u_b = state
        if last:
            u_a_next, u_b_next, g_a_next, g_b_next = zero, zero, zero, zero
        else:
            picked = strata_of(cell + 1)
            u_a_next, u_b_next = look("u_a", picked), look("u_b", picked)
            g_a_next, g_b_next = look("g_a", picked), look("g_b", picked)
        state_a, w, q, r = eliminate(state_a, "a", u_a + u_a_next, g_a_next)
        put("w_a", cell, w)
        put("q_a", cell, q)
        put("r_a", cell, r)
        state_b, w, q, r = eliminate(state_b, "b", u_b + u_b_next, g_b_next)
        put("w_b", cell, w)
        put("q_b", cell, q)
        put("r_b", cell, r)
        return state_a, state_b, u_a_next, u_b_next

    state = lax.fori_loop(0, CELLS - 1, forward, start, unroll=5)
    relation_a, relation_b, _, _ = forward(CELLS - 1, state, last=True)

    one = jnp.ones((ROWS, LANES), f32)

    def cumulate(step, state):
        q_a, w_a, q_b, w_b, c_ll, c_lr, c_rl, c_rr = state
        cell = CELLS - 1 - step
        eta = look("eta", strata_of(cell))
        put("eta", cell, eta)
        now = get("w_a", cell)
        q_a, w_a = now * q_a + get("q_a", cell), now * w_a
        now = get("w_b", cell)
        q_b, w_b = now * q_b + get("q_b", cell), now * w_b
        put("q_cum_a", cell, q_a)
        put("w_cum_a", cell, w_a)
        put("q_cum_b", cell, q_b)
        put("w_cum_b", cell, w_b)
        eta_q, eta_w = eta * q_a, eta * w_a
        return (
            q_a,
            w_a,
            q_b,
            w_b,
            c_ll + q_b * eta_q,
            c_lr + q_b * eta_w,
            c_rl + w_b * eta_q,
            c_rr + w_b * eta_w,
        )

    state = lax.fori_loop(
        0, CELLS, cumulate, (zero, one, zero, one, zero, zero, zero, zero), unroll=4
    )
    cross = state[4:]

    row = lax.broadcasted_iota(jnp.int32, (ROWS, LANES), 0)
    column = lax.broadcasted_iota(jnp.int32, (ROWS, LANES), 1)
    y_open = (row == PLANES - 1) | (row == ROWS - 1)
    z_last = column == LANES - 1
    z_open = z_last & (row >= PLANES)
    z_first = column == 0

    def next_y(x):
        return pltpu.roll(x, ROWS - 1, axis=0)

    def previous_y(x):
        return pltpu.roll(x, 1, axis=0)

    def next_z(x):
        moved = pltpu.roll(x, LANES - 1, axis=1)
        return jnp.where(z_last, pltpu.roll(moved, PLANES, axis=0), moved)

    def previous_z(x):
        moved = pltpu.roll(x, 1, axis=1)
        return jnp.where(z_first, pltpu.roll(moved, PLANES, axis=0), moved)

    def sources(cell, carry):
        picked = strata_of(cell)
        u_t = look("u_t", picked)
        h_y = jnp.where(y_open, 0.0, 1.0 / (u_t + next_y(u_t)))
        h_z = jnp.where(z_open, 0.0, 1.0 / (u_t + next_z(u_t)))
        por = look("por", picked)
        values = [conc_of(component, cell) for component in range(4)]
        mobile = []
        for component in range(2):
            x = values[component]
            flow_y = h_y * (next_y(x) - x)
            flow_z = h_z * (next_z(x) - x)
            flux = (flow_y - previous_y(flow_y)) + (flow_z - previous_z(flow_z))
            mobile.append(por * x + flux)
        put("s_a", cell, mobile[0] + look("src_a", picked) * values[2])
        put(
            "s_b",
            cell,
            mobile[1] + look("src_b", picked) * values[3] + look("src_ab", picked) * values[2],
        )
        return carry

    lax.fori_loop(0, CELLS, sources, 0, unroll=4)

    def edge_wait(side):
        pltpu.make_async_copy(
            edges.at[side], halo.at[side], edge_recv_sem.at[side]
        ).wait()

    for side in range(2):

        @pl.when(has_side[side])
        def _(side=side):
            edge_wait(side)
            rows = pl.ds(side * (PLANES - 1), CELLS, stride=PLANES)
            for half in range(HALVES):
                own = [edges[side, half, pl.ds(k * CELLS, CELLS), :] for k in range(3)]
                other = [halo[side, half, pl.ds(k * CELLS, CELLS), :] for k in range(3)]
                h = 1.0 / (own[0] + other[0])
                for component, name in ((1, "s_a"), (2, "s_b")):
                    spot_in = (FIELDS.index(name), half, rows, slice(None))
                    fields[spot_in] = fields[spot_in] + h * (other[component] - own[component])

    def source_forward(cell, state):
        j, j_left = state
        put("v_a", cell, get("r_a", cell) * j)
        j_left = j_left + get("q_a", cell) * j
        return get("s_a", cell + 1) + get("w_a", cell) * j, j_left

    j, j_left = lax.fori_loop(0, CELLS - 1, source_forward, (get("s_a", 0), zero), unroll=5)
    last_cell = CELLS - 1
    put("v_a", last_cell, get("r_a", last_cell) * j)
    j_left_a = j_left + get("q_a", last_cell) * j
    j_right_a = get("w_a", last_cell) * j

    def source_backward(step, state):
        p, j_left, j_right = state
        cell = CELLS - 1 - step
        p = get("w_a", cell) * p + get("v_a", cell)
        put("v_a", cell, p)
        forcing = get("s_b", cell) + get("eta", cell) * p
        put("s_b", cell, forcing)
        return p, j_left + get("q_cum_b", cell) * forcing, j_right + get("w_cum_b", cell) * forcing

    _, j_left_b, j_right_b = lax.fori_loop(0, CELLS, source_backward, (zero, zero, zero), unroll=4)

    k_a, alpha_a, delta_a = relation_a
    k_b, alpha_b, delta_b = relation_b
    parts = (
        k_a,
        alpha_a,
        delta_a,
        k_b,
        alpha_b,
        delta_b,
        *cross,
        j_left_a,
        j_right_a,
        j_left_b,
        j_right_b,
    )
    for index, part in enumerate(parts):
        send[pl.ds(index, ROWS, stride=SLOT), :] = part
    for index in range(len(parts), SLOT):
        send[pl.ds(index, ROWS, stride=SLOT), :] = zero

    def slot_of(index, size):
        return pl.ds(pl.multiple_of(index * size, 8), size)

    def outward(step, carry):
        peer = lax.rem(me + step, flow_size)
        pltpu.make_async_remote_copy(
            src_ref=send.at[slot_of(peer, SLOT)],
            dst_ref=recv.at[slot_of(me, SLOT)],
            send_sem=out_send_sem,
            recv_sem=out_recv_sem,
            device_id={"flow": peer},
            device_id_type=MESH,
        ).start()
        return carry

    lax.fori_loop(1, flow_size, outward, 0)
    recv[slot_of(me, SLOT), :] = send[slot_of(me, SLOT), :]

    def basis_forward(cell, state):
        j_0, j_l, j_r = state
        r, w = get("r_b", cell), get("w_b", cell)
        eta = get("eta", cell)
        j_0 = j_0 + get("s_b", cell)
        j_l = j_l + eta * get("q_cum_a", cell)
        j_r = j_r + eta * get("w_cum_a", cell)
        put("p_b", cell, r * j_0)
        put("y_l", cell, r * j_l)
        put("y_r", cell, r * j_r)
        return w * j_0, w * j_l, w * j_r

    lax.fori_loop(0, CELLS, basis_forward, (zero, zero, zero), unroll=4)

    def basis_backward(step, state):
        p, y_l, y_r = state
        cell = CELLS - 1 - step
        w = get("w_b", cell)
        p = w * p + get("p_b", cell)
        y_l = w * y_l + get("y_l", cell)
        y_r = w * y_r + get("y_r", cell)
        put("p_b", cell, p)
        put("y_l", cell, y_l)
        put("y_r", cell, y_r)
        picked = strata_of(cell)
        immobile_a, immobile_b = conc_of(2, cell), conc_of(3, cell)
        put("im_a", cell, look("im_a", picked) * immobile_a)
        put("ex_a", cell, look("ex_a", picked))
        put("im_b", cell, look("im_b", picked) * immobile_b + look("im_ab", picked) * immobile_a)
        put("ex_b", cell, look("ex_b", picked))
        put("ex_ab", cell, look("ex_ab", picked))
        return p, y_l, y_r

    lax.fori_loop(0, CELLS, basis_backward, (zero, zero, zero), unroll=4)

    def total_wait(src, dst, size, sem):
        span = pl.ds(0, (flow_size - 1) * size)
        pltpu.make_async_copy(src.at[span], dst.at[span], sem).wait()

    total_wait(send, recv, SLOT, out_recv_sem)

    (
        k_a,
        alpha_a,
        delta_a,
        k_b,
        alpha_b,
        delta_b,
        c_ll,
        c_lr,
        c_rl,
        c_rr,
        j_left_a,
        j_right_a,
        j_left_b,
        j_right_b,
    ) = [recv[pl.ds(index, ROWS, stride=SLOT), :] for index in range(14)]
    at_end = row == 0

    def up(x, shift):
        return pltpu.roll(x, ROWS - shift, axis=0)

    def down(x, shift):
        return pltpu.roll(x, shift, axis=0)

    def reduce_matrix(k, alpha, delta):
        h = 1.0 / (k + alpha)
        pull = k * h
        delta = delta + up(jnp.where(at_end, 0.0, alpha), 1)
        delta = delta + jnp.where(at_end, alpha * pull, 0.0)
        coupling = jnp.where(at_end, 0.0, k)
        levels = []
        shift = 1
        while shift < ROWS:
            ahead = up(coupling, shift)
            inverse = 1.0 / (coupling + ahead + delta)
            levels.append((shift, coupling, ahead, inverse))
            shed = delta * inverse
            delta = delta + coupling * down(shed, shift) + ahead * up(shed, shift)
            coupling = coupling * down(coupling * inverse, shift)
            shift *= 2
        return h, pull, levels, 1.0 / delta

    def reduce_source(reduced, k, j_left, j_right):
        h, pull, levels, inverse_delta = reduced
        j = j_right + up(jnp.where(at_end, 0.0, j_left), 1)
        j = j + jnp.where(at_end, pull * j_left, 0.0)
        for shift, coupling, ahead, inverse in levels:
            shed = j * inverse
            j = j + coupling * down(shed, shift) + ahead * up(shed, shift)
        right = j * inverse_delta
        left = jnp.where(at_end, h * (j_left + k * right), down(right, 1))
        return left, right

    reduced_a = reduce_matrix(k_a, alpha_a, delta_a)
    reduced_b = reduce_matrix(k_b, alpha_b, delta_b)
    left_a, right_a = reduce_source(reduced_a, k_a, j_left_a, j_right_a)
    left_b, right_b = reduce_source(
        reduced_b,
        k_b,
        j_left_b + c_ll * left_a + c_lr * right_a,
        j_right_b + c_rl * left_a + c_rr * right_a,
    )
    for index, part in enumerate((left_a, right_a, left_b, right_b)):
        back[pl.ds(index, ROWS, stride=BACK), :] = part
    for index in range(4, BACK):
        back[pl.ds(index, ROWS, stride=BACK), :] = zero

    def homeward(step, carry):
        peer = lax.rem(me + step, flow_size)
        pltpu.make_async_remote_copy(
            src_ref=back.at[slot_of(peer, BACK)],
            dst_ref=got.at[slot_of(me, BACK)],
            send_sem=back_send_sem,
            recv_sem=back_recv_sem,
            device_id={"flow": peer},
            device_id_type=MESH,
        ).start()
        return carry

    lax.fori_loop(1, flow_size, homeward, 0)
    got[slot_of(me, BACK), :] = back[slot_of(me, BACK), :]
    total_wait(back, got, BACK, back_recv_sem)
    left_a, right_a, left_b, right_b = [
        got[pl.ds(index, ROWS, stride=BACK), :] for index in range(4)
    ]

    def store(component, cell, value):
        rows = spot(component * CELLS + cell)
        for half in range(HALVES):
            piece = value[half * PLANES : (half + 1) * PLANES]
            out_ref[rows, pl.ds(half * LANES, LANES)] = piece

    def finish(cell, carry):
        a = get("v_a", cell) + get("q_cum_a", cell) * left_a + get("w_cum_a", cell) * right_a
        b = (
            get("p_b", cell)
            + get("q_cum_b", cell) * left_b
            + get("w_cum_b", cell) * right_b
            + get("y_l", cell) * left_a
            + get("y_r", cell) * right_a
        )
        store(0, cell, a)
        store(1, cell, b)
        store(2, cell, get("im_a", cell) + get("ex_a", cell) * a)
        store(3, cell, get("im_b", cell) + get("ex_b", cell) * b + get("ex_ab", cell) * a)
        return carry

    lax.fori_loop(0, CELLS, finish, 0, unroll=4)

    for side in range(2):

        @pl.when(has_side[side])
        def _(side=side):
            edge_copy(side).wait_send()

    total_wait(send, recv, SLOT, out_send_sem)
    total_wait(back, got, BACK, back_send_sem)


def per_device(
    flow_size,
    trans_size,
    concentration,
    stratum,
    porosity,
    dispersion_table,
    transverse_table,
    exchange_table,
    decay_table,
):
    f32 = jnp.float32
    components, cells, planes, width = concentration.shape
    total = components * cells * planes
    field_rows = cells * planes
    hbm = pl.BlockSpec(memory_space=pltpu.HBM)
    solved = pl.pallas_call(
        functools.partial(kernel, flow_size, trans_size),
        out_shape=jax.ShapeDtypeStruct((total, width), f32),
        in_specs=[hbm] * 7,
        out_specs=pl.BlockSpec(memory_space=pltpu.VMEM),
        scratch_shapes=[
            pltpu.SMEM((STRATA,), f32),
            pltpu.SMEM((2, STRATA), f32),
            pltpu.SMEM((STRATA,), f32),
            pltpu.SMEM((STRATA,), f32),
            pltpu.SMEM((STRATA,), f32),
            pltpu.VMEM((HALVES, total, LANES), f32),
            pltpu.VMEM((HALVES, field_rows, LANES), jnp.int32),
            pltpu.VMEM((len(TABLES), 8, LANES), f32),
            pltpu.VMEM((len(FIELDS), HALVES, field_rows, LANES), f32),
            pltpu.VMEM((2, HALVES, 3 * CELLS, LANES), f32),
            pltpu.VMEM((2, HALVES, 3 * CELLS, LANES), f32),
            pltpu.VMEM((flow_size * SLOT, LANES), f32),
            pltpu.VMEM((flow_size * SLOT, LANES), f32),
            pltpu.VMEM((flow_size * BACK, LANES), f32),
            pltpu.VMEM((flow_size * BACK, LANES), f32),
            pltpu.SemaphoreType.DMA((2 * HALVES + 5,)),
            pltpu.SemaphoreType.DMA((2,)),
            pltpu.SemaphoreType.DMA((2,)),
            pltpu.SemaphoreType.DMA,
            pltpu.SemaphoreType.DMA,
            pltpu.SemaphoreType.DMA,
            pltpu.SemaphoreType.DMA,
        ],
        compiler_params=pltpu.CompilerParams(
            collective_id=0, has_side_effects=True, vmem_limit_bytes=32 * 1024 * 1024
        ),
    )(
        *(
            pltpu.with_memory_space_constraint(x, pltpu.HBM)
            for x in (
                concentration.reshape(total, width),
                stratum.reshape(field_rows, width),
                porosity,
                dispersion_table.T,
                transverse_table,
                exchange_table,
                decay_table,
            )
        )
    )
    return solved.reshape(concentration.shape)


def solution(mesh):
    in_specs = (P(None, "flow", "trans", None), P("flow", "trans", None), P(), P(), P(), P(), P())
    out_specs = P(None, "flow", "trans", None)
    return jax.shard_map(
        functools.partial(per_device, mesh.shape["flow"], mesh.shape["trans"]),
        mesh=mesh,
        in_specs=in_specs,
        out_specs=out_specs,
        check_vma=False,
    )
```

```python
import functools
import itertools

import jax
import jax.numpy as jnp
from jax import lax
from jax.experimental import pallas as pl
from jax.experimental.pallas import tpu as pltpu
from jax.sharding import PartitionSpec as P

MESH = pl.DeviceIdType.MESH
STRATA = 16
CELLS = 16
PLANES = 16
LANES = 128
HALVES = 2
ROWS = HALVES * PLANES
SIDE = 4
CORES = 2
MATRIX = 10
SOURCE = 4
TABLES = (
    "u_a",
    "u_b",
    "u_t",
    "g_a",
    "g_b",
    "eta",
    "por",
    "src_a",
    "src_b",
    "src_ab",
    "im_a",
    "ex_a",
    "im_b",
    "ex_b",
    "im_ab",
    "ex_ab",
)
FIELDS = (
    "w_a",
    "q_a",
    "r_a",
    "w_b",
    "q_b",
    "r_b",
    "q_cum_a",
    "w_cum_a",
    "q_cum_b",
    "w_cum_b",
    "eta",
    "s_a",
    "s_b",
    "v_a",
    "v_b",
    "v_l",
    "v_r",
    "p_b",
    "y_l",
    "y_r",
    "im_a",
    "ex_a",
    "im_b",
    "ex_b",
    "ex_ab",
)


def kernel(
    flow_size,
    trans_size,
    conc_hbm,
    strat_hbm,
    por_hbm,
    disp_hbm,
    trans_hbm,
    exch_hbm,
    decay_hbm,
    out_ref,
    por_ref,
    disp_ref,
    trans_ref,
    exch_ref,
    decay_ref,
    conc,
    strat,
    tables,
    fields,
    edges,
    halo,
    matrix_out,
    matrix_in,
    source_out,
    source_in,
    back,
    got,
    load_sem,
    edge_send_sem,
    edge_recv_sem,
    matrix_send_sem,
    matrix_recv_sem,
    source_send_sem,
    source_recv_sem,
    back_send_sem,
    back_recv_sem,
):
    f32 = jnp.float32
    me = lax.axis_index("flow")
    group = lax.axis_index("trans")
    mobile_rows = 2 * CELLS * PLANES

    def load(source, target, rows, half, index):
        return pltpu.make_async_copy(
            source.at[rows, pl.ds(half * LANES, LANES)],
            target.at[half, rows],
            load_sem.at[index],
        )

    field_span = pl.ds(0, CELLS * PLANES)
    mobile_span = pl.ds(0, mobile_rows)
    immobile_span = pl.ds(mobile_rows, mobile_rows)
    first_loads, later_loads = [], []
    for half in range(HALVES):
        first_loads.append(load(strat_hbm, strat, field_span, half, half))
        first_loads.append(load(conc_hbm, conc, mobile_span, half, 2 + half))
        later_loads.append(load(conc_hbm, conc, immobile_span, half, 4 + half))
    table_loads = [
        pltpu.make_async_copy(src, dst, load_sem.at[6 + index])
        for index, (src, dst) in enumerate(
            (
                (por_hbm, por_ref),
                (disp_hbm, disp_ref),
                (trans_hbm, trans_ref),
                (exch_hbm, exch_ref),
                (decay_hbm, decay_ref),
            )
        )
    ]
    for copy in table_loads + first_loads + later_loads:
        copy.start()

    barrier = pltpu.get_barrier_semaphore()

    def greet(step, carry):
        peer = lax.rem(me + step, flow_size)
        pl.semaphore_signal(barrier, inc=1, device_id={"flow": peer}, device_id_type=MESH)
        return carry

    for step in (1, trans_size - 1):
        pl.semaphore_signal(
            barrier,
            inc=1,
            device_id={"trans": lax.rem(group + step, trans_size)},
            device_id_type=MESH,
        )
    lax.fori_loop(1, flow_size, greet, 0)

    lane = lax.broadcasted_iota(jnp.int32, (8, LANES), 1)

    def lane_table(read):
        table = jnp.full((8, LANES), read(0), f32)
        for stratum in range(1, STRATA):
            table = jnp.where(lane == stratum, read(stratum), table)
        return table

    for copy in table_loads:
        copy.wait()
    trans = lane_table(lambda k: trans_ref[k])
    tables[TABLES.index("u_t")] = 0.5 / trans

    def look(name, picked):
        table = tables[TABLES.index(name)]
        wide = jnp.concatenate([table] * (picked.shape[0] // 8), axis=0)
        return jnp.take_along_axis(wide, picked, axis=1, mode="promise_in_bounds")

    def spot(cell):
        start = cell * PLANES
        if not isinstance(cell, int):
            start = pl.multiple_of(start, PLANES)
        return pl.ds(start, PLANES)

    def strata_of(cell):
        return strat[:, spot(cell), :].reshape(ROWS, LANES)

    def conc_of(component, cell):
        return conc[:, spot(component * CELLS + cell), :].reshape(ROWS, LANES)

    def get(name, cell):
        return fields[FIELDS.index(name), :, spot(cell), :].reshape(ROWS, LANES)

    def put(name, cell, value):
        fields[FIELDS.index(name), :, spot(cell), :] = value.reshape(HALVES, PLANES, LANES)

    for copy in first_loads:
        copy.wait()

    for side, plane in ((0, 0), (1, PLANES - 1)):
        for half in range(HALVES):
            rows = pl.ds(plane, CELLS, stride=PLANES)
            picked = strat[half, rows, :]
            edges[side, half, pl.ds(0, CELLS), :] = look("u_t", picked)
            for component in range(2):
                rows = pl.ds(component * CELLS * PLANES + plane, CELLS, stride=PLANES)
                edges[side, half, pl.ds((component + 1) * CELLS, CELLS), :] = conc[half, rows, :]

    pl.semaphore_wait(barrier, flow_size + 1)

    def edge_copy(side):
        return pltpu.make_async_remote_copy(
            src_ref=edges.at[side],
            dst_ref=halo.at[1 - side],
            send_sem=edge_send_sem.at[side],
            recv_sem=edge_recv_sem.at[1 - side],
            device_id={"trans": group - 1 + 2 * side},
            device_id_type=MESH,
        )

    has_side = (group > 0, group < trans_size - 1)

    @pl.when(has_side[0])
    def _():
        edge_copy(0).start()

    @pl.when(has_side[1])
    def _():
        edge_copy(1).start()

    por = lane_table(lambda k: por_ref[k])
    disp_a = lane_table(lambda k: disp_ref[0, k])
    disp_b = lane_table(lambda k: disp_ref[1, k])
    exch = lane_table(lambda k: exch_ref[k])
    decay = lane_table(lambda k: decay_ref[k])
    rest = 1.0 - por
    m_a = 1.0 / (rest + exch + decay)
    m_b = 1.0 / (rest + exch)
    values = {
        "u_a": 0.5 / disp_a,
        "u_b": 0.5 / disp_b,
        "g_a": por + decay + exch * (rest + decay) * m_a,
        "g_b": por + exch * rest * m_b,
        "eta": decay + exch * exch * decay * m_a * m_b,
        "por": por,
        "src_a": exch * rest * m_a,
        "src_b": exch * rest * m_b,
        "src_ab": exch * m_b * decay * rest * m_a,
        "im_a": rest * m_a,
        "ex_a": exch * m_a,
        "im_b": rest * m_b,
        "ex_b": exch * m_b,
        "im_ab": decay * m_b * rest * m_a,
        "ex_ab": decay * m_b * exch * m_a,
    }
    for name, value in values.items():
        tables[TABLES.index(name)] = value

    def eliminate(state, name, r, g_next):
        k, alpha, delta = state
        w = 1.0 / (1.0 + r * (k + delta))
        rw = r * w
        q = rw * k
        return (k * w, alpha + q * delta, g_next + delta * w), w, q, rw

    first = strata_of(0)
    zero = jnp.zeros((ROWS, LANES), f32)
    u_a0, u_b0 = look("u_a", first), look("u_b", first)
    start = (
        (1.0 / u_a0, zero, look("g_a", first)),
        (1.0 / u_b0, zero, look("g_b", first)),
        u_a0,
        u_b0,
    )

    def forward(cell, state, last=False):
        state_a, state_b, u_a, u_b = state
        if last:
            u_a_next, u_b_next, g_a_next, g_b_next = zero, zero, zero, zero
        else:
            picked = strata_of(cell + 1)
            u_a_next, u_b_next = look("u_a", picked), look("u_b", picked)
            g_a_next, g_b_next = look("g_a", picked), look("g_b", picked)
        state_a, w, q, r = eliminate(state_a, "a", u_a + u_a_next, g_a_next)
        put("w_a", cell, w)
        put("q_a", cell, q)
        put("r_a", cell, r)
        state_b, w, q, r = eliminate(state_b, "b", u_b + u_b_next, g_b_next)
        put("w_b", cell, w)
        put("q_b", cell, q)
        put("r_b", cell, r)
        return state_a, state_b, u_a_next, u_b_next

    state = lax.fori_loop(0, CELLS - 1, forward, start, unroll=5)
    relation_a, relation_b, _, _ = forward(CELLS - 1, state, last=True)

    one = jnp.ones((ROWS, LANES), f32)

    def cumulate(step, state):
        q_a, w_a, q_b, w_b, c_ll, c_lr, c_rl, c_rr = state
        cell = CELLS - 1 - step
        eta = look("eta", strata_of(cell))
        put("eta", cell, eta)
        now = get("w_a", cell)
        q_a, w_a = now * q_a + get("q_a", cell), now * w_a
        now = get("w_b", cell)
        q_b, w_b = now * q_b + get("q_b", cell), now * w_b
        put("q_cum_a", cell, q_a)
        put("w_cum_a", cell, w_a)
        put("q_cum_b", cell, q_b)
        put("w_cum_b", cell, w_b)
        eta_q, eta_w = eta * q_a, eta * w_a
        return (
            q_a,
            w_a,
            q_b,
            w_b,
            c_ll + q_b * eta_q,
            c_lr + q_b * eta_w,
            c_rl + w_b * eta_q,
            c_rr + w_b * eta_w,
        )

    state = lax.fori_loop(
        0, CELLS, cumulate, (zero, one, zero, one, zero, zero, zero, zero), unroll=4
    )
    cross = state[4:]
    k_a, alpha_a, delta_a = relation_a
    k_b, alpha_b, delta_b = relation_b

    def exchange(source, target, send_sem, recv_sem, fan_out):
        def push(peer):
            pltpu.make_async_remote_copy(
                src_ref=source.at[peer],
                dst_ref=target.at[me],
                send_sem=send_sem,
                recv_sem=recv_sem,
                device_id={"flow": peer},
                device_id_type=MESH,
            ).start()

        fan_out(push)
        target[me] = source[me]

    def apart(offset):
        return min(offset[0], SIDE - offset[0]) + min(offset[1], SIDE - offset[1])

    offsets = sorted(
        itertools.product(range(SIDE), range(SIDE), range(CORES)), key=apart, reverse=True
    )
    place = (me // (SIDE * CORES), lax.rem(me // CORES, SIDE), lax.rem(me, CORES))

    def in_turn(push):
        for dz, dy, dc in offsets:
            if (dz, dy, dc) != (0, 0, 0):
                z = lax.rem(place[0] + dz, SIDE)
                y = lax.rem(place[1] + dy, SIDE)
                core = lax.rem(place[2] + dc, CORES)
                push((z * SIDE + y) * CORES + core)

    def total_wait(source, target, sem):
        span = pl.ds(0, flow_size - 1)
        pltpu.make_async_copy(source.at[span], target.at[span], sem).wait()

    for index, part in enumerate((k_a, alpha_a, delta_a, k_b, alpha_b, delta_b, *cross)):
        matrix_out[:, index, :] = part
    exchange(matrix_out, matrix_in, matrix_send_sem, matrix_recv_sem, in_turn)

    row = lax.broadcasted_iota(jnp.int32, (ROWS, LANES), 0)
    column = lax.broadcasted_iota(jnp.int32, (ROWS, LANES), 1)
    y_open = (row == PLANES - 1) | (row == ROWS - 1)
    z_last = column == LANES - 1
    z_open = z_last & (row >= PLANES)
    z_first = column == 0

    def next_y(x):
        return pltpu.roll(x, ROWS - 1, axis=0)

    def previous_y(x):
        return pltpu.roll(x, 1, axis=0)

    def next_z(x):
        moved = pltpu.roll(x, LANES - 1, axis=1)
        return jnp.where(z_last, pltpu.roll(moved, PLANES, axis=0), moved)

    def previous_z(x):
        moved = pltpu.roll(x, 1, axis=1)
        return jnp.where(z_first, pltpu.roll(moved, PLANES, axis=0), moved)

    def sources(cell, carry):
        picked = strata_of(cell)
        u_t = look("u_t", picked)
        h_y = jnp.where(y_open, 0.0, 1.0 / (u_t + next_y(u_t)))
        h_z = jnp.where(z_open, 0.0, 1.0 / (u_t + next_z(u_t)))
        por = look("por", picked)
        values = [conc_of(component, cell) for component in range(4)]
        mobile = []
        for component in range(2):
            x = values[component]
            flow_y = h_y * (next_y(x) - x)
            flow_z = h_z * (next_z(x) - x)
            flux = (flow_y - previous_y(flow_y)) + (flow_z - previous_z(flow_z))
            mobile.append(por * x + flux)
        put("s_a", cell, mobile[0] + look("src_a", picked) * values[2])
        put(
            "s_b",
            cell,
            mobile[1] + look("src_b", picked) * values[3] + look("src_ab", picked) * values[2],
        )
        return carry

    for copy in later_loads:
        copy.wait()
    lax.fori_loop(0, CELLS, sources, 0, unroll=4)

    def edge_wait(side):
        pltpu.make_async_copy(
            edges.at[side], halo.at[side], edge_recv_sem.at[side]
        ).wait()

    for side in range(2):

        @pl.when(has_side[side])
        def _(side=side):
            edge_wait(side)
            rows = pl.ds(side * (PLANES - 1), CELLS, stride=PLANES)
            for half in range(HALVES):
                own = [edges[side, half, pl.ds(k * CELLS, CELLS), :] for k in range(3)]
                other = [halo[side, half, pl.ds(k * CELLS, CELLS), :] for k in range(3)]
                h = 1.0 / (own[0] + other[0])
                for component, name in ((1, "s_a"), (2, "s_b")):
                    spot_in = (FIELDS.index(name), half, rows, slice(None))
                    fields[spot_in] = fields[spot_in] + h * (other[component] - own[component])

    def source_forward(cell, state):
        j, j_left = state
        put("v_a", cell, get("r_a", cell) * j)
        j_left = j_left + get("q_a", cell) * j
        return get("s_a", cell + 1) + get("w_a", cell) * j, j_left

    j, j_left = lax.fori_loop(0, CELLS - 1, source_forward, (get("s_a", 0), zero), unroll=5)
    last_cell = CELLS - 1
    put("v_a", last_cell, get("r_a", last_cell) * j)
    j_left_a = j_left + get("q_a", last_cell) * j
    j_right_a = get("w_a", last_cell) * j

    def source_backward(step, state):
        p, j_left, j_right = state
        cell = CELLS - 1 - step
        p = get("w_a", cell) * p + get("v_a", cell)
        put("v_a", cell, p)
        forcing = get("s_b", cell) + get("eta", cell) * p
        put("s_b", cell, forcing)
        return p, j_left + get("q_cum_b", cell) * forcing, j_right + get("w_cum_b", cell) * forcing

    _, j_left_b, j_right_b = lax.fori_loop(0, CELLS, source_backward, (zero, zero, zero), unroll=4)

    for index, part in enumerate((j_left_a, j_right_a, j_left_b, j_right_b)):
        source_out[:, index, :] = part
    exchange(source_out, source_in, source_send_sem, source_recv_sem, in_turn)

    def basis_forward(cell, state):
        j_0, j_l, j_r = state
        r, w = get("r_b", cell), get("w_b", cell)
        eta = get("eta", cell)
        j_0 = j_0 + get("s_b", cell)
        j_l = j_l + eta * get("q_cum_a", cell)
        j_r = j_r + eta * get("w_cum_a", cell)
        put("p_b", cell, r * j_0)
        put("y_l", cell, r * j_l)
        put("y_r", cell, r * j_r)
        return w * j_0, w * j_l, w * j_r

    lax.fori_loop(0, CELLS, basis_forward, (zero, zero, zero), unroll=4)

    def basis_backward(step, state):
        p, y_l, y_r = state
        cell = CELLS - 1 - step
        w = get("w_b", cell)
        p = w * p + get("p_b", cell)
        y_l = w * y_l + get("y_l", cell)
        y_r = w * y_r + get("y_r", cell)
        put("p_b", cell, p)
        put("y_l", cell, y_l)
        put("y_r", cell, y_r)
        picked = strata_of(cell)
        immobile_a, immobile_b = conc_of(2, cell), conc_of(3, cell)
        put("im_a", cell, look("im_a", picked) * immobile_a)
        put("ex_a", cell, look("ex_a", picked))
        put("im_b", cell, look("im_b", picked) * immobile_b + look("im_ab", picked) * immobile_a)
        put("ex_b", cell, look("ex_b", picked))
        put("ex_ab", cell, look("ex_ab", picked))
        return p, y_l, y_r

    lax.fori_loop(0, CELLS, basis_backward, (zero, zero, zero), unroll=4)

    total_wait(matrix_out, matrix_in, matrix_recv_sem)
    (
        k_a,
        alpha_a,
        delta_a,
        k_b,
        alpha_b,
        delta_b,
        c_ll,
        c_lr,
        c_rl,
        c_rr,
    ) = [matrix_in[:, index, :] for index in range(MATRIX)]
    at_end = row == 0

    def up(x, shift):
        return pltpu.roll(x, ROWS - shift, axis=0)

    def down(x, shift):
        return pltpu.roll(x, shift, axis=0)

    def reduce_matrix(k, alpha, delta):
        h = 1.0 / (k + alpha)
        pull = k * h
        delta = delta + up(jnp.where(at_end, 0.0, alpha), 1)
        delta = delta + jnp.where(at_end, alpha * pull, 0.0)
        coupling = jnp.where(at_end, 0.0, k)
        levels = []
        shift = 1
        while shift < ROWS:
            ahead = up(coupling, shift)
            inverse = 1.0 / (coupling + ahead + delta)
            levels.append((shift, coupling, ahead, inverse))
            shed = delta * inverse
            delta = delta + coupling * down(shed, shift) + ahead * up(shed, shift)
            coupling = coupling * down(coupling * inverse, shift)
            shift *= 2
        return h, pull, levels, 1.0 / delta

    def reduce_source(reduced, k, j_left, j_right):
        h, pull, levels, inverse_delta = reduced
        j = j_right + up(jnp.where(at_end, 0.0, j_left), 1)
        j = j + jnp.where(at_end, pull * j_left, 0.0)
        for shift, coupling, ahead, inverse in levels:
            shed = j * inverse
            j = j + coupling * down(shed, shift) + ahead * up(shed, shift)
        right = j * inverse_delta
        left = jnp.where(at_end, h * (j_left + k * right), down(right, 1))
        return left, right

    reduced_a = reduce_matrix(k_a, alpha_a, delta_a)
    reduced_b = reduce_matrix(k_b, alpha_b, delta_b)
    total_wait(source_out, source_in, source_recv_sem)
    j_left_a, j_right_a, j_left_b, j_right_b = [
        source_in[:, index, :] for index in range(SOURCE)
    ]
    left_a, right_a = reduce_source(reduced_a, k_a, j_left_a, j_right_a)
    left_b, right_b = reduce_source(
        reduced_b,
        k_b,
        j_left_b + c_ll * left_a + c_lr * right_a,
        j_right_b + c_rl * left_a + c_rr * right_a,
    )
    for index, part in enumerate((left_a, right_a, left_b, right_b)):
        back[:, index, :] = part
    exchange(back, got, back_send_sem, back_recv_sem, in_turn)
    total_wait(back, got, back_recv_sem)
    left_a, right_a, left_b, right_b = [got[:, index, :] for index in range(SOURCE)]

    def store(component, cell, value):
        rows = spot(component * CELLS + cell)
        for half in range(HALVES):
            piece = value[half * PLANES : (half + 1) * PLANES]
            out_ref[rows, pl.ds(half * LANES, LANES)] = piece

    def finish(cell, carry):
        a = get("v_a", cell) + get("q_cum_a", cell) * left_a + get("w_cum_a", cell) * right_a
        b = (
            get("p_b", cell)
            + get("q_cum_b", cell) * left_b
            + get("w_cum_b", cell) * right_b
            + get("y_l", cell) * left_a
            + get("y_r", cell) * right_a
        )
        store(0, cell, a)
        store(1, cell, b)
        store(2, cell, get("im_a", cell) + get("ex_a", cell) * a)
        store(3, cell, get("im_b", cell) + get("ex_b", cell) * b + get("ex_ab", cell) * a)
        return carry

    lax.fori_loop(0, CELLS, finish, 0, unroll=4)

    for side in range(2):

        @pl.when(has_side[side])
        def _(side=side):
            edge_copy(side).wait_send()

    total_wait(matrix_out, matrix_in, matrix_send_sem)
    total_wait(source_out, source_in, source_send_sem)
    total_wait(back, got, back_send_sem)


def per_device(
    flow_size,
    trans_size,
    concentration,
    stratum,
    porosity,
    dispersion_table,
    transverse_table,
    exchange_table,
    decay_table,
):
    f32 = jnp.float32
    components, cells, planes, width = concentration.shape
    total = components * cells * planes
    field_rows = cells * planes
    hbm = pl.BlockSpec(memory_space=pltpu.HBM)
    solved = pl.pallas_call(
        functools.partial(kernel, flow_size, trans_size),
        out_shape=jax.ShapeDtypeStruct((total, width), f32),
        in_specs=[hbm] * 7,
        out_specs=pl.BlockSpec(memory_space=pltpu.VMEM),
        scratch_shapes=[
            pltpu.SMEM((STRATA,), f32),
            pltpu.SMEM((2, STRATA), f32),
            pltpu.SMEM((STRATA,), f32),
            pltpu.SMEM((STRATA,), f32),
            pltpu.SMEM((STRATA,), f32),
            pltpu.VMEM((HALVES, total, LANES), f32),
            pltpu.VMEM((HALVES, field_rows, LANES), jnp.int32),
            pltpu.VMEM((len(TABLES), 8, LANES), f32),
            pltpu.VMEM((len(FIELDS), HALVES, field_rows, LANES), f32),
            pltpu.VMEM((2, HALVES, 3 * CELLS, LANES), f32),
            pltpu.VMEM((2, HALVES, 3 * CELLS, LANES), f32),
            pltpu.VMEM((flow_size, MATRIX, LANES), f32),
            pltpu.VMEM((flow_size, MATRIX, LANES), f32),
            pltpu.VMEM((flow_size, SOURCE, LANES), f32),
            pltpu.VMEM((flow_size, SOURCE, LANES), f32),
            pltpu.VMEM((flow_size, SOURCE, LANES), f32),
            pltpu.VMEM((flow_size, SOURCE, LANES), f32),
            pltpu.SemaphoreType.DMA((11,)),
            pltpu.SemaphoreType.DMA((2,)),
            pltpu.SemaphoreType.DMA((2,)),
            pltpu.SemaphoreType.DMA,
            pltpu.SemaphoreType.DMA,
            pltpu.SemaphoreType.DMA,
            pltpu.SemaphoreType.DMA,
            pltpu.SemaphoreType.DMA,
            pltpu.SemaphoreType.DMA,
        ],
        compiler_params=pltpu.CompilerParams(
            collective_id=0, has_side_effects=True, vmem_limit_bytes=32 * 1024 * 1024
        ),
    )(
        *(
            pltpu.with_memory_space_constraint(x, pltpu.HBM)
            for x in (
                concentration.reshape(total, width),
                stratum.reshape(field_rows, width),
                porosity,
                dispersion_table.T,
                transverse_table,
                exchange_table,
                decay_table,
            )
        )
    )
    return solved.reshape(concentration.shape)


def solution(mesh):
    in_specs = (P(None, "flow", "trans", None), P("flow", "trans", None), P(), P(), P(), P(), P())
    out_specs = P(None, "flow", "trans", None)
    return jax.shard_map(
        functools.partial(per_device, mesh.shape["flow"], mesh.shape["trans"]),
        mesh=mesh,
        in_specs=in_specs,
        out_specs=out_specs,
        check_vma=False,
    )
```

```python
import functools
import itertools

import jax
import jax.numpy as jnp
from jax import lax
from jax.experimental import pallas as pl
from jax.experimental.pallas import tpu as pltpu
from jax.sharding import PartitionSpec as P

MESH = pl.DeviceIdType.MESH
STRATA = 16
CELLS = 16
PLANES = 16
LANES = 128
HALVES = 2
ROWS = HALVES * PLANES
CHUNK = 8
SIDE = 4
CORES = 2
MATRIX = 10
SOURCE = 4
TABLES = (
    "u_a",
    "u_b",
    "u_t",
    "g_a",
    "g_b",
    "eta",
    "por",
    "src_a",
    "src_b",
    "src_ab",
    "im_a",
    "ex_a",
    "im_b",
    "ex_b",
    "im_ab",
    "ex_ab",
)
FIELDS = (
    "w_a",
    "q_a",
    "r_a",
    "w_b",
    "q_b",
    "r_b",
    "q_cum_a",
    "w_cum_a",
    "q_cum_b",
    "w_cum_b",
    "eta",
    "s_a",
    "s_b",
    "v_a",
    "v_b",
    "v_l",
    "v_r",
    "p_b",
    "y_l",
    "y_r",
    "im_a",
    "ex_a",
    "im_b",
    "ex_b",
    "ex_ab",
)


def kernel(
    flow_size,
    trans_size,
    conc_hbm,
    strat_hbm,
    por_hbm,
    disp_hbm,
    trans_hbm,
    exch_hbm,
    decay_hbm,
    fields,
    ends,
    por_ref,
    disp_ref,
    trans_ref,
    exch_ref,
    decay_ref,
    conc,
    strat,
    tables,
    edges,
    halo,
    matrix_out,
    matrix_in,
    source_out,
    source_in,
    back,
    got,
    load_sem,
    edge_send_sem,
    edge_recv_sem,
    matrix_send_sem,
    matrix_recv_sem,
    source_send_sem,
    source_recv_sem,
    back_send_sem,
    back_recv_sem,
):
    f32 = jnp.float32
    me = lax.axis_index("flow")
    group = lax.axis_index("trans")
    def apart(offset):
        return min(offset[0], SIDE - offset[0]) + min(offset[1], SIDE - offset[1])

    offsets = sorted(
        itertools.product(range(SIDE), range(SIDE), range(CORES)), key=apart, reverse=True
    )
    place = (me // (SIDE * CORES), lax.rem(me // CORES, SIDE), lax.rem(me, CORES))

    def in_turn(push):
        for dz, dy, dc in offsets:
            if (dz, dy, dc) != (0, 0, 0):
                z = lax.rem(place[0] + dz, SIDE)
                y = lax.rem(place[1] + dy, SIDE)
                core = lax.rem(place[2] + dc, CORES)
                push((z * SIDE + y) * CORES + core)

    barrier = pltpu.get_barrier_semaphore()

    def greet(peer):
        pl.semaphore_signal(barrier, inc=1, device_id={"flow": peer}, device_id_type=MESH)

    in_turn(greet)
    for step in (1, trans_size - 1):
        pl.semaphore_signal(
            barrier,
            inc=1,
            device_id={"trans": lax.rem(group + step, trans_size)},
            device_id_type=MESH,
        )
    mobile_rows = 2 * CELLS * PLANES

    def load(source, target, rows, half, index):
        return pltpu.make_async_copy(
            source.at[rows, pl.ds(half * LANES, LANES)],
            target.at[half, rows],
            load_sem.at[index],
        )

    field_span = pl.ds(0, CELLS * PLANES)
    mobile_span = pl.ds(0, mobile_rows)
    immobile_span = pl.ds(mobile_rows, mobile_rows)
    first_loads, later_loads = [], []
    for half in range(HALVES):
        first_loads.append(load(strat_hbm, strat, field_span, half, half))
        first_loads.append(load(conc_hbm, conc, mobile_span, half, 2 + half))
        later_loads.append(load(conc_hbm, conc, immobile_span, half, 4 + half))
    table_loads = [
        pltpu.make_async_copy(src, dst, load_sem.at[6 + index])
        for index, (src, dst) in enumerate(
            (
                (por_hbm, por_ref),
                (disp_hbm, disp_ref),
                (trans_hbm, trans_ref),
                (exch_hbm, exch_ref),
                (decay_hbm, decay_ref),
            )
        )
    ]
    for copy in table_loads + first_loads + later_loads:
        copy.start()

    lane = lax.broadcasted_iota(jnp.int32, (8, LANES), 1)

    def lane_table(read):
        table = jnp.full((8, LANES), read(0), f32)
        for stratum in range(1, STRATA):
            table = jnp.where(lane == stratum, read(stratum), table)
        return table

    for copy in table_loads:
        copy.wait()
    trans = lane_table(lambda k: trans_ref[k])
    tables[TABLES.index("u_t")] = 0.5 / trans

    def look(name, picked):
        table = tables[TABLES.index(name)]
        wide = jnp.concatenate([table] * (picked.shape[0] // 8), axis=0)
        return jnp.take_along_axis(wide, picked, axis=1, mode="promise_in_bounds")

    def spot(cell):
        start = cell * PLANES
        if not isinstance(cell, int):
            start = pl.multiple_of(start, PLANES)
        return pl.ds(start, PLANES)

    def strata_of(cell):
        return strat[:, spot(cell), :].reshape(ROWS, LANES)

    def conc_of(component, cell):
        return conc[:, spot(component * CELLS + cell), :].reshape(ROWS, LANES)

    def get(name, cell):
        return fields[FIELDS.index(name), :, spot(cell), :].reshape(ROWS, LANES)

    def put(name, cell, value):
        fields[FIELDS.index(name), :, spot(cell), :] = value.reshape(HALVES, PLANES, LANES)

    for copy in first_loads:
        copy.wait()

    for side, plane in ((0, 0), (1, PLANES - 1)):
        for half in range(HALVES):
            rows = pl.ds(plane, CELLS, stride=PLANES)
            picked = strat[half, rows, :]
            edges[side, half, pl.ds(0, CELLS), :] = look("u_t", picked)
            for component in range(2):
                rows = pl.ds(component * CELLS * PLANES + plane, CELLS, stride=PLANES)
                edges[side, half, pl.ds((component + 1) * CELLS, CELLS), :] = conc[half, rows, :]

    por = lane_table(lambda k: por_ref[k])
    disp_a = lane_table(lambda k: disp_ref[0, k])
    disp_b = lane_table(lambda k: disp_ref[1, k])
    exch = lane_table(lambda k: exch_ref[k])
    decay = lane_table(lambda k: decay_ref[k])
    rest = 1.0 - por
    m_a = 1.0 / (rest + exch + decay)
    m_b = 1.0 / (rest + exch)
    values = {
        "u_a": 0.5 / disp_a,
        "u_b": 0.5 / disp_b,
        "g_a": por + decay + exch * (rest + decay) * m_a,
        "g_b": por + exch * rest * m_b,
        "eta": decay + exch * exch * decay * m_a * m_b,
        "por": por,
        "src_a": exch * rest * m_a,
        "src_b": exch * rest * m_b,
        "src_ab": exch * m_b * decay * rest * m_a,
        "im_a": rest * m_a,
        "ex_a": exch * m_a,
        "im_b": rest * m_b,
        "ex_b": exch * m_b,
        "im_ab": decay * m_b * rest * m_a,
        "ex_ab": decay * m_b * exch * m_a,
    }
    for name, value in values.items():
        tables[TABLES.index(name)] = value

    def eliminate(state, name, r, g_next):
        k, alpha, delta = state
        w = 1.0 / (1.0 + r * (k + delta))
        rw = r * w
        q = rw * k
        return (k * w, alpha + q * delta, g_next + delta * w), w, q, rw

    first = strata_of(0)
    zero = jnp.zeros((ROWS, LANES), f32)
    u_a0, u_b0 = look("u_a", first), look("u_b", first)
    start = (
        (1.0 / u_a0, zero, look("g_a", first)),
        (1.0 / u_b0, zero, look("g_b", first)),
        u_a0,
        u_b0,
    )

    def forward(cell, state, last=False):
        state_a, state_b, u_a, u_b = state
        if last:
            u_a_next, u_b_next, g_a_next, g_b_next = zero, zero, zero, zero
        else:
            picked = strata_of(cell + 1)
            u_a_next, u_b_next = look("u_a", picked), look("u_b", picked)
            g_a_next, g_b_next = look("g_a", picked), look("g_b", picked)
        state_a, w, q, r = eliminate(state_a, "a", u_a + u_a_next, g_a_next)
        put("w_a", cell, w)
        put("q_a", cell, q)
        put("r_a", cell, r)
        state_b, w, q, r = eliminate(state_b, "b", u_b + u_b_next, g_b_next)
        put("w_b", cell, w)
        put("q_b", cell, q)
        put("r_b", cell, r)
        return state_a, state_b, u_a_next, u_b_next

    state = lax.fori_loop(0, CELLS - 1, forward, start, unroll=5)
    relation_a, relation_b, _, _ = forward(CELLS - 1, state, last=True)

    one = jnp.ones((ROWS, LANES), f32)

    def cumulate(step, state):
        q_a, w_a, q_b, w_b, c_ll, c_lr, c_rl, c_rr = state
        cell = CELLS - 1 - step
        eta = look("eta", strata_of(cell))
        put("eta", cell, eta)
        now = get("w_a", cell)
        q_a, w_a = now * q_a + get("q_a", cell), now * w_a
        now = get("w_b", cell)
        q_b, w_b = now * q_b + get("q_b", cell), now * w_b
        put("q_cum_a", cell, q_a)
        put("w_cum_a", cell, w_a)
        put("q_cum_b", cell, q_b)
        put("w_cum_b", cell, w_b)
        eta_q, eta_w = eta * q_a, eta * w_a
        return (
            q_a,
            w_a,
            q_b,
            w_b,
            c_ll + q_b * eta_q,
            c_lr + q_b * eta_w,
            c_rl + w_b * eta_q,
            c_rr + w_b * eta_w,
        )

    state = lax.fori_loop(
        0, CELLS, cumulate, (zero, one, zero, one, zero, zero, zero, zero), unroll=4
    )
    cross = state[4:]
    pl.semaphore_wait(barrier, flow_size + 1)

    def edge_copy(side):
        return pltpu.make_async_remote_copy(
            src_ref=edges.at[side],
            dst_ref=halo.at[1 - side],
            send_sem=edge_send_sem.at[side],
            recv_sem=edge_recv_sem.at[1 - side],
            device_id={"trans": group - 1 + 2 * side},
            device_id_type=MESH,
        )

    has_side = (group > 0, group < trans_size - 1)

    @pl.when(has_side[0])
    def _():
        edge_copy(0).start()

    @pl.when(has_side[1])
    def _():
        edge_copy(1).start()

    k_a, alpha_a, delta_a = relation_a
    k_b, alpha_b, delta_b = relation_b

    def exchange(source, target, send_sem, recv_sem, fan_out):
        def push(peer):
            pltpu.make_async_remote_copy(
                src_ref=source.at[peer],
                dst_ref=target.at[me],
                send_sem=send_sem,
                recv_sem=recv_sem,
                device_id={"flow": peer},
                device_id_type=MESH,
            ).start()

        fan_out(push)
        target[me] = source[me]

    def total_wait(source, target, sem):
        span = pl.ds(0, flow_size - 1)
        pltpu.make_async_copy(source.at[span], target.at[span], sem).wait()

    for index, part in enumerate((k_a, alpha_a, delta_a, k_b, alpha_b, delta_b, *cross)):
        matrix_out[:, index, :] = part
    exchange(matrix_out, matrix_in, matrix_send_sem, matrix_recv_sem, in_turn)

    row = lax.broadcasted_iota(jnp.int32, (ROWS, LANES), 0)
    column = lax.broadcasted_iota(jnp.int32, (ROWS, LANES), 1)
    z_last = column == LANES - 1
    z_open = z_last & (row >= PLANES)
    z_first = column == 0

    def swap(x):
        return jnp.concatenate([x[PLANES:], x[:PLANES]], axis=0)

    def next_z(x):
        moved = pltpu.roll(x, LANES - 1, axis=1)
        return jnp.where(z_last, swap(moved), moved)

    def previous_z(x):
        moved = pltpu.roll(x, 1, axis=1)
        return jnp.where(z_first, swap(moved), moved)

    def across(start):
        return pl.ds(start, CELLS, stride=PLANES)

    def strata_plane(plane):
        return jnp.concatenate([strat[half, across(plane), :] for half in range(HALVES)], axis=0)

    def conc_plane(component, plane):
        rows = across(component * CELLS * PLANES + plane)
        return jnp.concatenate([conc[half, rows, :] for half in range(HALVES)], axis=0)

    def put_plane(name, plane, value):
        for half in range(HALVES):
            piece = value[half * CELLS : (half + 1) * CELLS]
            fields[FIELDS.index(name), half, across(plane), :] = piece

    def sources(plane, state):
        picked, u_t, mobile, arriving = state
        ahead = plane + 1 - (plane + 1) // PLANES
        picked_ahead = strata_plane(ahead)
        u_ahead = look("u_t", picked_ahead)
        mobile_ahead = [conc_plane(component, ahead) for component in range(2)]
        h_y = 1.0 / (u_t + u_ahead)
        h_z = jnp.where(z_open, 0.0, 1.0 / (u_t + next_z(u_t)))
        por = look("por", picked)
        leaving, filled = [], []
        for component in range(2):
            x = mobile[component]
            flow_y = h_y * (mobile_ahead[component] - x)
            flow_z = h_z * (next_z(x) - x)
            flux = (flow_y - arriving[component]) + (flow_z - previous_z(flow_z))
            leaving.append(flow_y)
            filled.append(por * x + flux)
        immobile_a, immobile_b = conc_plane(2, plane), conc_plane(3, plane)
        put_plane("s_a", plane, filled[0] + look("src_a", picked) * immobile_a)
        put_plane(
            "s_b",
            plane,
            filled[1] + look("src_b", picked) * immobile_b + look("src_ab", picked) * immobile_a,
        )
        return picked_ahead, u_ahead, mobile_ahead, leaving

    for copy in later_loads:
        copy.wait()
    picked = strata_plane(0)
    start = (
        picked,
        look("u_t", picked),
        [conc_plane(component, 0) for component in range(2)],
        [zero, zero],
    )
    lax.fori_loop(0, PLANES, sources, start, unroll=2)

    def edge_wait(side):
        pltpu.make_async_copy(
            edges.at[side], halo.at[side], edge_recv_sem.at[side]
        ).wait()

    for side in range(2):

        @pl.when(has_side[side])
        def _(side=side):
            edge_wait(side)
            rows = pl.ds(side * (PLANES - 1), CELLS, stride=PLANES)
            for half in range(HALVES):
                own = [edges[side, half, pl.ds(k * CELLS, CELLS), :] for k in range(3)]
                other = [halo[side, half, pl.ds(k * CELLS, CELLS), :] for k in range(3)]
                h = 1.0 / (own[0] + other[0])
                for component, name in ((1, "s_a"), (2, "s_b")):
                    spot_in = (FIELDS.index(name), half, rows, slice(None))
                    fields[spot_in] = fields[spot_in] + h * (other[component] - own[component])

    def source_forward(cell, state):
        j, j_left = state
        put("v_a", cell, get("r_a", cell) * j)
        j_left = j_left + get("q_a", cell) * j
        return get("s_a", cell + 1) + get("w_a", cell) * j, j_left

    j, j_left = lax.fori_loop(0, CELLS - 1, source_forward, (get("s_a", 0), zero), unroll=5)
    last_cell = CELLS - 1
    put("v_a", last_cell, get("r_a", last_cell) * j)
    j_left_a = j_left + get("q_a", last_cell) * j
    j_right_a = get("w_a", last_cell) * j

    def source_backward(step, state):
        p, j_left, j_right = state
        cell = CELLS - 1 - step
        p = get("w_a", cell) * p + get("v_a", cell)
        put("v_a", cell, p)
        forcing = get("s_b", cell) + get("eta", cell) * p
        put("s_b", cell, forcing)
        return p, j_left + get("q_cum_b", cell) * forcing, j_right + get("w_cum_b", cell) * forcing

    _, j_left_b, j_right_b = lax.fori_loop(0, CELLS, source_backward, (zero, zero, zero), unroll=4)

    for index, part in enumerate((j_left_a, j_right_a, j_left_b, j_right_b)):
        source_out[:, index, :] = part
    exchange(source_out, source_in, source_send_sem, source_recv_sem, in_turn)

    def basis_forward(cell, state):
        j_0, j_l, j_r = state
        r, w = get("r_b", cell), get("w_b", cell)
        eta = get("eta", cell)
        j_0 = j_0 + get("s_b", cell)
        j_l = j_l + eta * get("q_cum_a", cell)
        j_r = j_r + eta * get("w_cum_a", cell)
        put("p_b", cell, r * j_0)
        put("y_l", cell, r * j_l)
        put("y_r", cell, r * j_r)
        return w * j_0, w * j_l, w * j_r

    lax.fori_loop(0, CELLS, basis_forward, (zero, zero, zero), unroll=4)

    def basis_backward(step, state):
        p, y_l, y_r = state
        cell = CELLS - 1 - step
        w = get("w_b", cell)
        p = w * p + get("p_b", cell)
        y_l = w * y_l + get("y_l", cell)
        y_r = w * y_r + get("y_r", cell)
        put("p_b", cell, p)
        put("y_l", cell, y_l)
        put("y_r", cell, y_r)
        picked = strata_of(cell)
        immobile_a, immobile_b = conc_of(2, cell), conc_of(3, cell)
        put("im_a", cell, look("im_a", picked) * immobile_a)
        put("ex_a", cell, look("ex_a", picked))
        put("im_b", cell, look("im_b", picked) * immobile_b + look("im_ab", picked) * immobile_a)
        put("ex_b", cell, look("ex_b", picked))
        put("ex_ab", cell, look("ex_ab", picked))
        return p, y_l, y_r

    lax.fori_loop(0, CELLS, basis_backward, (zero, zero, zero), unroll=4)

    total_wait(matrix_out, matrix_in, matrix_recv_sem)
    (
        k_a,
        alpha_a,
        delta_a,
        k_b,
        alpha_b,
        delta_b,
        c_ll,
        c_lr,
        c_rl,
        c_rr,
    ) = [matrix_in[:, index, :] for index in range(MATRIX)]
    at_end = row == 0

    def up(x, shift):
        if shift % 8 == 0:
            return jnp.concatenate([x[shift:], x[:shift]], axis=0)
        return pltpu.roll(x, ROWS - shift, axis=0)

    def down(x, shift):
        if shift % 8 == 0:
            return jnp.concatenate([x[ROWS - shift :], x[: ROWS - shift]], axis=0)
        return pltpu.roll(x, shift, axis=0)

    def reduce_matrix(k, alpha, delta):
        h = 1.0 / (k + alpha)
        pull = k * h
        delta = delta + up(jnp.where(at_end, 0.0, alpha), 1)
        delta = delta + jnp.where(at_end, alpha * pull, 0.0)
        coupling = jnp.where(at_end, 0.0, k)
        levels = []
        shift = 1
        while shift < ROWS:
            ahead = up(coupling, shift)
            inverse = 1.0 / (coupling + ahead + delta)
            levels.append((shift, coupling, ahead, inverse))
            shed = delta * inverse
            delta = delta + coupling * down(shed, shift) + ahead * up(shed, shift)
            coupling = coupling * down(coupling * inverse, shift)
            shift *= 2
        return h, pull, levels, 1.0 / delta

    def reduce_source(reduced, k, j_left, j_right):
        h, pull, levels, inverse_delta = reduced
        j = j_right + up(jnp.where(at_end, 0.0, j_left), 1)
        j = j + jnp.where(at_end, pull * j_left, 0.0)
        for shift, coupling, ahead, inverse in levels:
            shed = j * inverse
            j = j + coupling * down(shed, shift) + ahead * up(shed, shift)
        right = j * inverse_delta
        left = jnp.where(at_end, h * (j_left + k * right), down(right, 1))
        return left, right

    reduced_a = reduce_matrix(k_a, alpha_a, delta_a)
    reduced_b = reduce_matrix(k_b, alpha_b, delta_b)
    total_wait(source_out, source_in, source_recv_sem)
    j_left_a, j_right_a, j_left_b, j_right_b = [
        source_in[:, index, :] for index in range(SOURCE)
    ]
    left_a, right_a = reduce_source(reduced_a, k_a, j_left_a, j_right_a)
    left_b, right_b = reduce_source(
        reduced_b,
        k_b,
        j_left_b + c_ll * left_a + c_lr * right_a,
        j_right_b + c_rl * left_a + c_rr * right_a,
    )
    for index, part in enumerate((left_a, right_a, left_b, right_b)):
        back[:, index, :] = part
    exchange(back, got, back_send_sem, back_recv_sem, in_turn)
    total_wait(back, got, back_recv_sem)
    for index in range(SOURCE):
        ends[index] = got[:, index, :]

    for side in range(2):

        @pl.when(has_side[side])
        def _(side=side):
            edge_copy(side).wait_send()

    total_wait(matrix_out, matrix_in, matrix_send_sem)
    total_wait(source_out, source_in, source_send_sem)
    total_wait(back, got, back_send_sem)


def spread(start, size):
    return pl.ds(pl.multiple_of(start, PLANES), size)


def finish(fields, ends, out_hbm, out, out_sem):
    left_a, right_a, left_b, right_b = [ends[index] for index in range(SOURCE)]

    def get(name, cell):
        rows = spread(cell * PLANES, PLANES)
        return fields[FIELDS.index(name), :, rows, :].reshape(ROWS, LANES)

    def store(component, cell, value):
        rows = spread((component * CELLS + cell) * PLANES, PLANES)
        for half in range(HALVES):
            piece = value[half * PLANES : (half + 1) * PLANES]
            out[rows, pl.ds(half * LANES, LANES)] = piece

    def leave(chunk, component):
        rows = spread((component * CELLS + chunk * CHUNK) * PLANES, CHUNK * PLANES)
        return pltpu.make_async_copy(
            out.at[rows], out_hbm.at[rows], out_sem.at[chunk * 4 + component]
        )

    def fill(chunk, carry):
        for step in range(CHUNK):
            cell = chunk * CHUNK + step
            a = get("v_a", cell) + get("q_cum_a", cell) * left_a + get("w_cum_a", cell) * right_a
            b = (
                get("p_b", cell)
                + get("q_cum_b", cell) * left_b
                + get("w_cum_b", cell) * right_b
                + get("y_l", cell) * left_a
                + get("y_r", cell) * right_a
            )
            store(0, cell, a)
            store(1, cell, b)
            store(2, cell, get("im_a", cell) + get("ex_a", cell) * a)
            store(3, cell, get("im_b", cell) + get("ex_b", cell) * b + get("ex_ab", cell) * a)
        for component in range(4):
            leave(chunk, component).start()
        return carry

    def settle(chunk, carry):
        for component in range(4):
            leave(chunk, component).wait()
        return carry

    lax.fori_loop(0, CELLS // CHUNK, fill, 0)
    lax.fori_loop(0, CELLS // CHUNK, settle, 0)


def per_device(
    flow_size,
    trans_size,
    concentration,
    stratum,
    porosity,
    dispersion_table,
    transverse_table,
    exchange_table,
    decay_table,
):
    f32 = jnp.float32
    components, cells, planes, width = concentration.shape
    total = components * cells * planes
    field_rows = cells * planes
    hbm = pl.BlockSpec(memory_space=pltpu.HBM)
    vmem = pl.BlockSpec(memory_space=pltpu.VMEM)
    fields, ends = pl.pallas_call(
        functools.partial(kernel, flow_size, trans_size),
        out_shape=(
            jax.ShapeDtypeStruct((len(FIELDS), HALVES, field_rows, LANES), f32),
            jax.ShapeDtypeStruct((SOURCE, ROWS, LANES), f32),
        ),
        in_specs=[hbm] * 7,
        out_specs=(vmem, vmem),
        scratch_shapes=[
            pltpu.SMEM((STRATA,), f32),
            pltpu.SMEM((2, STRATA), f32),
            pltpu.SMEM((STRATA,), f32),
            pltpu.SMEM((STRATA,), f32),
            pltpu.SMEM((STRATA,), f32),
            pltpu.VMEM((HALVES, total, LANES), f32),
            pltpu.VMEM((HALVES, field_rows, LANES), jnp.int32),
            pltpu.VMEM((len(TABLES), 8, LANES), f32),
            pltpu.VMEM((2, HALVES, 3 * CELLS, LANES), f32),
            pltpu.VMEM((2, HALVES, 3 * CELLS, LANES), f32),
            pltpu.VMEM((flow_size, MATRIX, LANES), f32),
            pltpu.VMEM((flow_size, MATRIX, LANES), f32),
            pltpu.VMEM((flow_size, SOURCE, LANES), f32),
            pltpu.VMEM((flow_size, SOURCE, LANES), f32),
            pltpu.VMEM((flow_size, SOURCE, LANES), f32),
            pltpu.VMEM((flow_size, SOURCE, LANES), f32),
            pltpu.SemaphoreType.DMA((11,)),
            pltpu.SemaphoreType.DMA((2,)),
            pltpu.SemaphoreType.DMA((2,)),
            pltpu.SemaphoreType.DMA,
            pltpu.SemaphoreType.DMA,
            pltpu.SemaphoreType.DMA,
            pltpu.SemaphoreType.DMA,
            pltpu.SemaphoreType.DMA,
            pltpu.SemaphoreType.DMA,
        ],
        compiler_params=pltpu.CompilerParams(
            collective_id=0, has_side_effects=True, vmem_limit_bytes=32 * 1024 * 1024
        ),
    )(
        *(
            pltpu.with_memory_space_constraint(x, pltpu.HBM)
            for x in (
                concentration.reshape(total, width),
                stratum.reshape(field_rows, width),
                porosity,
                dispersion_table.T,
                transverse_table,
                exchange_table,
                decay_table,
            )
        )
    )
    solved = pl.pallas_call(
        finish,
        out_shape=jax.ShapeDtypeStruct((total, width), f32),
        in_specs=[vmem, vmem],
        out_specs=hbm,
        scratch_shapes=[
            pltpu.VMEM((total, width), f32),
            pltpu.SemaphoreType.DMA((4 * CELLS // CHUNK,)),
        ],
        compiler_params=pltpu.CompilerParams(vmem_limit_bytes=16 * 1024 * 1024),
    )(
        pltpu.with_memory_space_constraint(fields, pltpu.VMEM),
        pltpu.with_memory_space_constraint(ends, pltpu.VMEM),
    )
    return solved.reshape(concentration.shape)


def solution(mesh):
    in_specs = (P(None, "flow", "trans", None), P("flow", "trans", None), P(), P(), P(), P(), P())
    out_specs = P(None, "flow", "trans", None)
    return jax.shard_map(
        functools.partial(per_device, mesh.shape["flow"], mesh.shape["trans"]),
        mesh=mesh,
        in_specs=in_specs,
        out_specs=out_specs,
        check_vma=False,
    )
```

```python
import functools
import itertools

import jax
import jax.numpy as jnp
from jax import lax
from jax.experimental import pallas as pl
from jax.experimental.pallas import tpu as pltpu
from jax.sharding import PartitionSpec as P

MESH = pl.DeviceIdType.MESH
STRATA = 16
CELLS = 16
PLANES = 16
LANES = 128
HALVES = 2
ROWS = HALVES * PLANES
CHUNK = 8
SIDE = 4
CORES = 2
EDGE_ROWS = (0, PLANES - 1, PLANES, ROWS - 1)
MATRIX = 10
SOURCE = 4
TABLES = (
    "u_a",
    "u_b",
    "u_t",
    "g_a",
    "g_b",
    "eta",
    "por",
    "src_a",
    "src_b",
    "src_ab",
    "im_a",
    "ex_a",
    "im_b",
    "ex_b",
    "im_ab",
    "ex_ab",
)
FIELDS = (
    "w_a",
    "q_a",
    "r_a",
    "w_b",
    "q_b",
    "r_b",
    "q_cum_a",
    "w_cum_a",
    "q_cum_b",
    "w_cum_b",
    "eta",
    "s_a",
    "s_b",
    "v_a",
    "v_b",
    "v_l",
    "v_r",
    "p_b",
    "y_l",
    "y_r",
    "im_a",
    "ex_a",
    "im_b",
    "ex_b",
    "ex_ab",
)


def kernel(
    flow_size,
    trans_size,
    conc_hbm,
    strat_hbm,
    por_hbm,
    disp_hbm,
    trans_hbm,
    exch_hbm,
    decay_hbm,
    fields,
    ends,
    por_ref,
    disp_ref,
    trans_ref,
    exch_ref,
    decay_ref,
    conc,
    strat,
    tables,
    edges,
    halo,
    matrix_out,
    matrix_in,
    source_out,
    edge_out,
    source_in,
    back,
    got,
    load_sem,
    edge_send_sem,
    edge_recv_sem,
    matrix_send_sem,
    matrix_recv_sem,
    source_send_sem,
    source_recv_sem,
    back_send_sem,
    back_recv_sem,
):
    f32 = jnp.float32
    me = lax.axis_index("flow")
    group = lax.axis_index("trans")
    def apart(offset):
        return min(offset[0], SIDE - offset[0]) + min(offset[1], SIDE - offset[1])

    offsets = sorted(
        itertools.product(range(SIDE), range(SIDE), range(CORES)), key=apart, reverse=True
    )
    place = (me // (SIDE * CORES), lax.rem(me // CORES, SIDE), lax.rem(me, CORES))

    def in_turn(push):
        for dz, dy, dc in offsets:
            if (dz, dy, dc) != (0, 0, 0):
                z = lax.rem(place[0] + dz, SIDE)
                y = lax.rem(place[1] + dy, SIDE)
                core = lax.rem(place[2] + dc, CORES)
                push((z * SIDE + y) * CORES + core)

    barrier = pltpu.get_barrier_semaphore()

    def greet(peer):
        pl.semaphore_signal(barrier, inc=1, device_id={"flow": peer}, device_id_type=MESH)

    in_turn(greet)
    for step in (1, trans_size - 1):
        pl.semaphore_signal(
            barrier,
            inc=1,
            device_id={"trans": lax.rem(group + step, trans_size)},
            device_id_type=MESH,
        )
    mobile_rows = 2 * CELLS * PLANES

    def load(source, target, rows, half, index):
        return pltpu.make_async_copy(
            source.at[rows, pl.ds(half * LANES, LANES)],
            target.at[half, rows],
            load_sem.at[index],
        )

    field_span = pl.ds(0, CELLS * PLANES)
    mobile_span = pl.ds(0, mobile_rows)
    immobile_span = pl.ds(mobile_rows, mobile_rows)
    first_loads, later_loads = [], []
    for half in range(HALVES):
        first_loads.append(load(strat_hbm, strat, field_span, half, half))
        first_loads.append(load(conc_hbm, conc, mobile_span, half, 2 + half))
        later_loads.append(load(conc_hbm, conc, immobile_span, half, 4 + half))
    table_loads = [
        pltpu.make_async_copy(src, dst, load_sem.at[6 + index])
        for index, (src, dst) in enumerate(
            (
                (por_hbm, por_ref),
                (disp_hbm, disp_ref),
                (trans_hbm, trans_ref),
                (exch_hbm, exch_ref),
                (decay_hbm, decay_ref),
            )
        )
    ]
    for copy in table_loads + first_loads + later_loads:
        copy.start()

    lane = lax.broadcasted_iota(jnp.int32, (8, LANES), 1)

    def lane_table(read):
        table = jnp.full((8, LANES), read(0), f32)
        for stratum in range(1, STRATA):
            table = jnp.where(lane == stratum, read(stratum), table)
        return table

    for copy in table_loads:
        copy.wait()
    trans = lane_table(lambda k: trans_ref[k])
    tables[TABLES.index("u_t")] = 0.5 / trans

    def look(name, picked):
        table = tables[TABLES.index(name)]
        wide = jnp.concatenate([table] * (picked.shape[0] // 8), axis=0)
        return jnp.take_along_axis(wide, picked, axis=1, mode="promise_in_bounds")

    def spot(cell):
        start = cell * PLANES
        if not isinstance(cell, int):
            start = pl.multiple_of(start, PLANES)
        return pl.ds(start, PLANES)

    def strata_of(cell):
        return strat[:, spot(cell), :].reshape(ROWS, LANES)

    def conc_of(component, cell):
        return conc[:, spot(component * CELLS + cell), :].reshape(ROWS, LANES)

    def get(name, cell):
        return fields[FIELDS.index(name), :, spot(cell), :].reshape(ROWS, LANES)

    def put(name, cell, value):
        fields[FIELDS.index(name), :, spot(cell), :] = value.reshape(HALVES, PLANES, LANES)

    for copy in first_loads:
        copy.wait()

    for side, plane in ((0, 0), (1, PLANES - 1)):
        for half in range(HALVES):
            rows = pl.ds(plane, CELLS, stride=PLANES)
            picked = strat[half, rows, :]
            edges[side, half, pl.ds(0, CELLS), :] = look("u_t", picked)
            for component in range(2):
                rows = pl.ds(component * CELLS * PLANES + plane, CELLS, stride=PLANES)
                edges[side, half, pl.ds((component + 1) * CELLS, CELLS), :] = conc[half, rows, :]

    por = lane_table(lambda k: por_ref[k])
    disp_a = lane_table(lambda k: disp_ref[0, k])
    disp_b = lane_table(lambda k: disp_ref[1, k])
    exch = lane_table(lambda k: exch_ref[k])
    decay = lane_table(lambda k: decay_ref[k])
    rest = 1.0 - por
    m_a = 1.0 / (rest + exch + decay)
    m_b = 1.0 / (rest + exch)
    values = {
        "u_a": 0.5 / disp_a,
        "u_b": 0.5 / disp_b,
        "g_a": por + decay + exch * (rest + decay) * m_a,
        "g_b": por + exch * rest * m_b,
        "eta": decay + exch * exch * decay * m_a * m_b,
        "por": por,
        "src_a": exch * rest * m_a,
        "src_b": exch * rest * m_b,
        "src_ab": exch * m_b * decay * rest * m_a,
        "im_a": rest * m_a,
        "ex_a": exch * m_a,
        "im_b": rest * m_b,
        "ex_b": exch * m_b,
        "im_ab": decay * m_b * rest * m_a,
        "ex_ab": decay * m_b * exch * m_a,
    }
    for name, value in values.items():
        tables[TABLES.index(name)] = value

    def eliminate(state, name, r, g_next):
        k, alpha, delta = state
        w = 1.0 / (1.0 + r * (k + delta))
        rw = r * w
        q = rw * k
        return (k * w, alpha + q * delta, g_next + delta * w), w, q, rw

    first = strata_of(0)
    zero = jnp.zeros((ROWS, LANES), f32)
    u_a0, u_b0 = look("u_a", first), look("u_b", first)
    start = (
        (1.0 / u_a0, zero, look("g_a", first)),
        (1.0 / u_b0, zero, look("g_b", first)),
        u_a0,
        u_b0,
    )

    def forward(cell, state, last=False):
        state_a, state_b, u_a, u_b = state
        if last:
            u_a_next, u_b_next, g_a_next, g_b_next = zero, zero, zero, zero
        else:
            picked = strata_of(cell + 1)
            u_a_next, u_b_next = look("u_a", picked), look("u_b", picked)
            g_a_next, g_b_next = look("g_a", picked), look("g_b", picked)
        state_a, w, q, r = eliminate(state_a, "a", u_a + u_a_next, g_a_next)
        put("w_a", cell, w)
        put("q_a", cell, q)
        put("r_a", cell, r)
        state_b, w, q, r = eliminate(state_b, "b", u_b + u_b_next, g_b_next)
        put("w_b", cell, w)
        put("q_b", cell, q)
        put("r_b", cell, r)
        return state_a, state_b, u_a_next, u_b_next

    state = lax.fori_loop(0, CELLS - 1, forward, start, unroll=5)
    relation_a, relation_b, _, _ = forward(CELLS - 1, state, last=True)

    one = jnp.ones((ROWS, LANES), f32)

    def cumulate(step, state):
        q_a, w_a, q_b, w_b, c_ll, c_lr, c_rl, c_rr = state
        cell = CELLS - 1 - step
        eta = look("eta", strata_of(cell))
        put("eta", cell, eta)
        now = get("w_a", cell)
        q_a, w_a = now * q_a + get("q_a", cell), now * w_a
        now = get("w_b", cell)
        q_b, w_b = now * q_b + get("q_b", cell), now * w_b
        put("q_cum_a", cell, q_a)
        put("w_cum_a", cell, w_a)
        put("q_cum_b", cell, q_b)
        put("w_cum_b", cell, w_b)
        eta_q, eta_w = eta * q_a, eta * w_a
        return (
            q_a,
            w_a,
            q_b,
            w_b,
            c_ll + q_b * eta_q,
            c_lr + q_b * eta_w,
            c_rl + w_b * eta_q,
            c_rr + w_b * eta_w,
        )

    state = lax.fori_loop(
        0, CELLS, cumulate, (zero, one, zero, one, zero, zero, zero, zero), unroll=4
    )
    cross = state[4:]
    pl.semaphore_wait(barrier, flow_size + 1)

    def edge_copy(side):
        return pltpu.make_async_remote_copy(
            src_ref=edges.at[side],
            dst_ref=halo.at[1 - side],
            send_sem=edge_send_sem.at[side],
            recv_sem=edge_recv_sem.at[1 - side],
            device_id={"trans": group - 1 + 2 * side},
            device_id_type=MESH,
        )

    has_side = (group > 0, group < trans_size - 1)

    @pl.when(has_side[0])
    def _():
        edge_copy(0).start()

    @pl.when(has_side[1])
    def _():
        edge_copy(1).start()

    k_a, alpha_a, delta_a = relation_a
    k_b, alpha_b, delta_b = relation_b

    def exchange(source, target, send_sem, recv_sem, fan_out):
        def push(peer):
            pltpu.make_async_remote_copy(
                src_ref=source.at[peer],
                dst_ref=target.at[me],
                send_sem=send_sem,
                recv_sem=recv_sem,
                device_id={"flow": peer},
                device_id_type=MESH,
            ).start()

        fan_out(push)
        target[me] = source[me]

    def total_wait(source, target, sem):
        span = pl.ds(0, flow_size - 1)
        pltpu.make_async_copy(source.at[span], target.at[span], sem).wait()

    for index, part in enumerate((k_a, alpha_a, delta_a, k_b, alpha_b, delta_b, *cross)):
        matrix_out[:, index, :] = part
    exchange(matrix_out, matrix_in, matrix_send_sem, matrix_recv_sem, in_turn)

    row = lax.broadcasted_iota(jnp.int32, (ROWS, LANES), 0)
    column = lax.broadcasted_iota(jnp.int32, (ROWS, LANES), 1)
    z_last = column == LANES - 1
    z_open = z_last & (row >= PLANES)
    z_first = column == 0

    def swap(x):
        return jnp.concatenate([x[PLANES:], x[:PLANES]], axis=0)

    def next_z(x):
        moved = pltpu.roll(x, LANES - 1, axis=1)
        return jnp.where(z_last, swap(moved), moved)

    def previous_z(x):
        moved = pltpu.roll(x, 1, axis=1)
        return jnp.where(z_first, swap(moved), moved)

    def across(start):
        return pl.ds(start, CELLS, stride=PLANES)

    def strata_plane(plane):
        return jnp.concatenate([strat[half, across(plane), :] for half in range(HALVES)], axis=0)

    def conc_plane(component, plane):
        rows = across(component * CELLS * PLANES + plane)
        return jnp.concatenate([conc[half, rows, :] for half in range(HALVES)], axis=0)

    def put_plane(name, plane, value):
        for half in range(HALVES):
            piece = value[half * CELLS : (half + 1) * CELLS]
            fields[FIELDS.index(name), half, across(plane), :] = piece

    def sources(plane, state):
        picked, u_t, mobile, arriving = state
        ahead = plane + 1 - (plane + 1) // PLANES
        picked_ahead = strata_plane(ahead)
        u_ahead = look("u_t", picked_ahead)
        mobile_ahead = [conc_plane(component, ahead) for component in range(2)]
        h_y = 1.0 / (u_t + u_ahead)
        h_z = jnp.where(z_open, 0.0, 1.0 / (u_t + next_z(u_t)))
        por = look("por", picked)
        leaving, filled = [], []
        for component in range(2):
            x = mobile[component]
            flow_y = h_y * (mobile_ahead[component] - x)
            flow_z = h_z * (next_z(x) - x)
            flux = (flow_y - arriving[component]) + (flow_z - previous_z(flow_z))
            leaving.append(flow_y)
            filled.append(por * x + flux)
        immobile_a, immobile_b = conc_plane(2, plane), conc_plane(3, plane)
        put_plane("s_a", plane, filled[0] + look("src_a", picked) * immobile_a)
        put_plane(
            "s_b",
            plane,
            filled[1] + look("src_b", picked) * immobile_b + look("src_ab", picked) * immobile_a,
        )
        return picked_ahead, u_ahead, mobile_ahead, leaving

    for copy in later_loads:
        copy.wait()
    picked = strata_plane(0)
    start = (
        picked,
        look("u_t", picked),
        [conc_plane(component, 0) for component in range(2)],
        [zero, zero],
    )
    lax.fori_loop(0, PLANES, sources, start, unroll=2)

    def source_forward(cell, state):
        j, j_left = state
        put("v_a", cell, get("r_a", cell) * j)
        j_left = j_left + get("q_a", cell) * j
        return get("s_a", cell + 1) + get("w_a", cell) * j, j_left

    last_cell = CELLS - 1

    def totals(keep):
        j, j_left = lax.fori_loop(
            0, last_cell, source_forward, (get("s_a", 0), zero), unroll=5
        )
        put("v_a", last_cell, get("r_a", last_cell) * j)
        j_left_a = j_left + get("q_a", last_cell) * j
        j_right_a = get("w_a", last_cell) * j

        def source_backward(step, state):
            p, j_left, j_right = state
            cell = CELLS - 1 - step
            p = get("w_a", cell) * p + get("v_a", cell)
            forcing = get("s_b", cell) + get("eta", cell) * p
            if keep:
                put("v_a", cell, p)
                put("s_b", cell, forcing)
            j_left = j_left + get("q_cum_b", cell) * forcing
            return p, j_left, j_right + get("w_cum_b", cell) * forcing

        _, j_left_b, j_right_b = lax.fori_loop(
            0, CELLS, source_backward, (zero, zero, zero), unroll=4
        )
        return j_left_a, j_right_a, j_left_b, j_right_b

    def post(source, peer):
        pltpu.make_async_remote_copy(
            src_ref=source,
            dst_ref=source_in.at[me],
            send_sem=source_send_sem,
            recv_sem=source_recv_sem,
            device_id={"flow": peer},
            device_id_type=MESH,
        ).start()

    def is_inner(peer):
        place_in_half = lax.rem(peer, PLANES)
        return (place_in_half > 0) & (place_in_half < PLANES - 1)

    for index, part in enumerate(totals(keep=False)):
        source_out[:, index, :] = part

    def post_inner(peer):
        @pl.when(is_inner(peer))
        def _():
            post(source_out.at[peer], peer)

    in_turn(post_inner)

    @pl.when(is_inner(me))
    def _():
        source_in[me] = source_out[me]

    def edge_wait(side):
        pltpu.make_async_copy(
            edges.at[side], halo.at[side], edge_recv_sem.at[side]
        ).wait()

    for side in range(2):

        @pl.when(has_side[side])
        def _(side=side):
            edge_wait(side)
            rows = pl.ds(side * (PLANES - 1), CELLS, stride=PLANES)
            for half in range(HALVES):
                own = [edges[side, half, pl.ds(k * CELLS, CELLS), :] for k in range(3)]
                other = [halo[side, half, pl.ds(k * CELLS, CELLS), :] for k in range(3)]
                h = 1.0 / (own[0] + other[0])
                for component, name in ((1, "s_a"), (2, "s_b")):
                    spot_in = (FIELDS.index(name), half, rows, slice(None))
                    fields[spot_in] = fields[spot_in] + h * (other[component] - own[component])

    for index, part in enumerate(totals(keep=True)):
        for position, edge_row in enumerate(EDGE_ROWS):
            edge_out[position, index : index + 1, :] = part[edge_row : edge_row + 1]
    for position, edge_row in enumerate(EDGE_ROWS):

        @pl.when(me != edge_row)
        def _(position=position, edge_row=edge_row):
            post(edge_out.at[position], edge_row)

    for position, edge_row in enumerate(EDGE_ROWS):

        @pl.when(me == edge_row)
        def _(position=position):
            source_in[me] = edge_out[position]

    def basis_forward(cell, state):
        j_0, j_l, j_r = state
        r, w = get("r_b", cell), get("w_b", cell)
        eta = get("eta", cell)
        j_0 = j_0 + get("s_b", cell)
        j_l = j_l + eta * get("q_cum_a", cell)
        j_r = j_r + eta * get("w_cum_a", cell)
        put("p_b", cell, r * j_0)
        put("y_l", cell, r * j_l)
        put("y_r", cell, r * j_r)
        return w * j_0, w * j_l, w * j_r

    lax.fori_loop(0, CELLS, basis_forward, (zero, zero, zero), unroll=4)

    def basis_backward(step, state):
        p, y_l, y_r = state
        cell = CELLS - 1 - step
        w = get("w_b", cell)
        p = w * p + get("p_b", cell)
        y_l = w * y_l + get("y_l", cell)
        y_r = w * y_r + get("y_r", cell)
        put("p_b", cell, p)
        put("y_l", cell, y_l)
        put("y_r", cell, y_r)
        picked = strata_of(cell)
        immobile_a, immobile_b = conc_of(2, cell), conc_of(3, cell)
        put("im_a", cell, look("im_a", picked) * immobile_a)
        put("ex_a", cell, look("ex_a", picked))
        put("im_b", cell, look("im_b", picked) * immobile_b + look("im_ab", picked) * immobile_a)
        put("ex_b", cell, look("ex_b", picked))
        put("ex_ab", cell, look("ex_ab", picked))
        return p, y_l, y_r

    lax.fori_loop(0, CELLS, basis_backward, (zero, zero, zero), unroll=4)

    total_wait(matrix_out, matrix_in, matrix_recv_sem)
    (
        k_a,
        alpha_a,
        delta_a,
        k_b,
        alpha_b,
        delta_b,
        c_ll,
        c_lr,
        c_rl,
        c_rr,
    ) = [matrix_in[:, index, :] for index in range(MATRIX)]
    at_end = row == 0

    def up(x, shift):
        if shift % 8 == 0:
            return jnp.concatenate([x[shift:], x[:shift]], axis=0)
        return pltpu.roll(x, ROWS - shift, axis=0)

    def down(x, shift):
        if shift % 8 == 0:
            return jnp.concatenate([x[ROWS - shift :], x[: ROWS - shift]], axis=0)
        return pltpu.roll(x, shift, axis=0)

    def reduce_matrix(k, alpha, delta):
        h = 1.0 / (k + alpha)
        pull = k * h
        delta = delta + up(jnp.where(at_end, 0.0, alpha), 1)
        delta = delta + jnp.where(at_end, alpha * pull, 0.0)
        coupling = jnp.where(at_end, 0.0, k)
        levels = []
        shift = 1
        while shift < ROWS:
            ahead = up(coupling, shift)
            inverse = 1.0 / (coupling + ahead + delta)
            levels.append((shift, coupling, ahead, inverse))
            shed = delta * inverse
            delta = delta + coupling * down(shed, shift) + ahead * up(shed, shift)
            coupling = coupling * down(coupling * inverse, shift)
            shift *= 2
        return h, pull, levels, 1.0 / delta

    def reduce_source(reduced, k, j_left, j_right):
        h, pull, levels, inverse_delta = reduced
        j = j_right + up(jnp.where(at_end, 0.0, j_left), 1)
        j = j + jnp.where(at_end, pull * j_left, 0.0)
        for shift, coupling, ahead, inverse in levels:
            shed = j * inverse
            j = j + coupling * down(shed, shift) + ahead * up(shed, shift)
        right = j * inverse_delta
        left = jnp.where(at_end, h * (j_left + k * right), down(right, 1))
        return left, right

    reduced_a = reduce_matrix(k_a, alpha_a, delta_a)
    reduced_b = reduce_matrix(k_b, alpha_b, delta_b)
    total_wait(source_out, source_in, source_recv_sem)
    j_left_a, j_right_a, j_left_b, j_right_b = [
        source_in[:, index, :] for index in range(SOURCE)
    ]
    left_a, right_a = reduce_source(reduced_a, k_a, j_left_a, j_right_a)
    left_b, right_b = reduce_source(
        reduced_b,
        k_b,
        j_left_b + c_ll * left_a + c_lr * right_a,
        j_right_b + c_rl * left_a + c_rr * right_a,
    )
    for index, part in enumerate((left_a, right_a, left_b, right_b)):
        back[:, index, :] = part
    exchange(back, got, back_send_sem, back_recv_sem, in_turn)
    total_wait(back, got, back_recv_sem)
    for index in range(SOURCE):
        ends[index] = got[:, index, :]

    for side in range(2):

        @pl.when(has_side[side])
        def _(side=side):
            edge_copy(side).wait_send()

    total_wait(matrix_out, matrix_in, matrix_send_sem)
    total_wait(source_out, source_in, source_send_sem)
    total_wait(back, got, back_send_sem)


def spread(start, size):
    return pl.ds(pl.multiple_of(start, PLANES), size)


def finish(fields, ends, out_hbm, out, out_sem):
    left_a, right_a, left_b, right_b = [ends[index] for index in range(SOURCE)]

    def get(name, cell):
        rows = spread(cell * PLANES, PLANES)
        return fields[FIELDS.index(name), :, rows, :].reshape(ROWS, LANES)

    def store(component, cell, value):
        rows = spread((component * CELLS + cell) * PLANES, PLANES)
        for half in range(HALVES):
            piece = value[half * PLANES : (half + 1) * PLANES]
            out[rows, pl.ds(half * LANES, LANES)] = piece

    def leave(chunk, component):
        rows = spread((component * CELLS + chunk * CHUNK) * PLANES, CHUNK * PLANES)
        return pltpu.make_async_copy(
            out.at[rows], out_hbm.at[rows], out_sem.at[chunk * 4 + component]
        )

    def fill(chunk, carry):
        for step in range(CHUNK):
            cell = chunk * CHUNK + step
            a = get("v_a", cell) + get("q_cum_a", cell) * left_a + get("w_cum_a", cell) * right_a
            b = (
                get("p_b", cell)
                + get("q_cum_b", cell) * left_b
                + get("w_cum_b", cell) * right_b
                + get("y_l", cell) * left_a
                + get("y_r", cell) * right_a
            )
            store(0, cell, a)
            store(1, cell, b)
            store(2, cell, get("im_a", cell) + get("ex_a", cell) * a)
            store(3, cell, get("im_b", cell) + get("ex_b", cell) * b + get("ex_ab", cell) * a)
        for component in range(4):
            leave(chunk, component).start()
        return carry

    def settle(chunk, carry):
        for component in range(4):
            leave(chunk, component).wait()
        return carry

    lax.fori_loop(0, CELLS // CHUNK, fill, 0)
    lax.fori_loop(0, CELLS // CHUNK, settle, 0)


def per_device(
    flow_size,
    trans_size,
    concentration,
    stratum,
    porosity,
    dispersion_table,
    transverse_table,
    exchange_table,
    decay_table,
):
    f32 = jnp.float32
    components, cells, planes, width = concentration.shape
    total = components * cells * planes
    field_rows = cells * planes
    hbm = pl.BlockSpec(memory_space=pltpu.HBM)
    vmem = pl.BlockSpec(memory_space=pltpu.VMEM)
    fields, ends = pl.pallas_call(
        functools.partial(kernel, flow_size, trans_size),
        out_shape=(
            jax.ShapeDtypeStruct((len(FIELDS), HALVES, field_rows, LANES), f32),
            jax.ShapeDtypeStruct((SOURCE, ROWS, LANES), f32),
        ),
        in_specs=[hbm] * 7,
        out_specs=(vmem, vmem),
        scratch_shapes=[
            pltpu.SMEM((STRATA,), f32),
            pltpu.SMEM((2, STRATA), f32),
            pltpu.SMEM((STRATA,), f32),
            pltpu.SMEM((STRATA,), f32),
            pltpu.SMEM((STRATA,), f32),
            pltpu.VMEM((HALVES, total, LANES), f32),
            pltpu.VMEM((HALVES, field_rows, LANES), jnp.int32),
            pltpu.VMEM((len(TABLES), 8, LANES), f32),
            pltpu.VMEM((2, HALVES, 3 * CELLS, LANES), f32),
            pltpu.VMEM((2, HALVES, 3 * CELLS, LANES), f32),
            pltpu.VMEM((flow_size, MATRIX, LANES), f32),
            pltpu.VMEM((flow_size, MATRIX, LANES), f32),
            pltpu.VMEM((flow_size, SOURCE, LANES), f32),
            pltpu.VMEM((len(EDGE_ROWS), SOURCE, LANES), f32),
            pltpu.VMEM((flow_size, SOURCE, LANES), f32),
            pltpu.VMEM((flow_size, SOURCE, LANES), f32),
            pltpu.VMEM((flow_size, SOURCE, LANES), f32),
            pltpu.SemaphoreType.DMA((11,)),
            pltpu.SemaphoreType.DMA((2,)),
            pltpu.SemaphoreType.DMA((2,)),
            pltpu.SemaphoreType.DMA,
            pltpu.SemaphoreType.DMA,
            pltpu.SemaphoreType.DMA,
            pltpu.SemaphoreType.DMA,
            pltpu.SemaphoreType.DMA,
            pltpu.SemaphoreType.DMA,
        ],
        compiler_params=pltpu.CompilerParams(
            collective_id=0, has_side_effects=True, vmem_limit_bytes=32 * 1024 * 1024
        ),
    )(
        *(
            pltpu.with_memory_space_constraint(x, pltpu.HBM)
            for x in (
                concentration.reshape(total, width),
                stratum.reshape(field_rows, width),
                porosity,
                dispersion_table.T,
                transverse_table,
                exchange_table,
                decay_table,
            )
        )
    )
    solved = pl.pallas_call(
        finish,
        out_shape=jax.ShapeDtypeStruct((total, width), f32),
        in_specs=[vmem, vmem],
        out_specs=hbm,
        scratch_shapes=[
            pltpu.VMEM((total, width), f32),
            pltpu.SemaphoreType.DMA((4 * CELLS // CHUNK,)),
        ],
        compiler_params=pltpu.CompilerParams(vmem_limit_bytes=16 * 1024 * 1024),
    )(
        pltpu.with_memory_space_constraint(fields, pltpu.VMEM),
        pltpu.with_memory_space_constraint(ends, pltpu.VMEM),
    )
    return solved.reshape(concentration.shape)


def solution(mesh):
    in_specs = (P(None, "flow", "trans", None), P("flow", "trans", None), P(), P(), P(), P(), P())
    out_specs = P(None, "flow", "trans", None)
    return jax.shard_map(
        functools.partial(per_device, mesh.shape["flow"], mesh.shape["trans"]),
        mesh=mesh,
        in_specs=in_specs,
        out_specs=out_specs,
        check_vma=False,
    )
```

```python
import functools
import itertools

import jax
import jax.numpy as jnp
from jax import lax
from jax.experimental import pallas as pl
from jax.experimental.pallas import tpu as pltpu
from jax.sharding import PartitionSpec as P

MESH = pl.DeviceIdType.MESH
STRATA = 16
CELLS = 16
PLANES = 16
LANES = 128
HALVES = 2
ROWS = HALVES * PLANES
CHUNK = 8
SIDE = 4
CORES = 2
EDGE_ROWS = (0, PLANES - 1, PLANES, ROWS - 1)
MATRIX = 10
SOURCE = 4
TABLES = (
    "u_a",
    "u_b",
    "u_t",
    "g_a",
    "g_b",
    "eta",
    "por",
    "src_a",
    "src_b",
    "src_ab",
    "im_a",
    "ex_a",
    "im_b",
    "ex_b",
    "im_ab",
    "ex_ab",
)
FIELDS = (
    "w_a",
    "q_a",
    "r_a",
    "w_b",
    "q_b",
    "r_b",
    "q_cum_a",
    "w_cum_a",
    "q_cum_b",
    "w_cum_b",
    "eta",
    "s_a",
    "s_b",
    "v_a",
    "v_b",
    "v_l",
    "v_r",
    "p_b",
    "y_l",
    "y_r",
    "im_a",
    "ex_a",
    "im_b",
    "ex_b",
    "ex_ab",
)


def kernel(
    flow_size,
    trans_size,
    conc_hbm,
    strat_hbm,
    por_hbm,
    disp_hbm,
    trans_hbm,
    exch_hbm,
    decay_hbm,
    fields,
    ends,
    por_ref,
    disp_ref,
    trans_ref,
    exch_ref,
    decay_ref,
    conc,
    strat,
    tables,
    edges,
    halo,
    matrix_out,
    matrix_in,
    source_out,
    edge_out,
    source_in,
    back,
    got,
    load_sem,
    edge_send_sem,
    edge_recv_sem,
    matrix_send_sem,
    matrix_recv_sem,
    source_send_sem,
    source_recv_sem,
    back_send_sem,
    back_recv_sem,
):
    f32 = jnp.float32
    me = lax.axis_index("flow")
    group = lax.axis_index("trans")
    def apart(offset):
        return min(offset[0], SIDE - offset[0]) + min(offset[1], SIDE - offset[1])

    offsets = sorted(
        itertools.product(range(SIDE), range(SIDE), range(CORES)), key=apart, reverse=True
    )
    place = (me // (SIDE * CORES), lax.rem(me // CORES, SIDE), lax.rem(me, CORES))

    def in_turn(push):
        for dz, dy, dc in offsets:
            if (dz, dy, dc) != (0, 0, 0):
                z = lax.rem(place[0] + dz, SIDE)
                y = lax.rem(place[1] + dy, SIDE)
                core = lax.rem(place[2] + dc, CORES)
                push((z * SIDE + y) * CORES + core)

    barrier = pltpu.get_barrier_semaphore()

    def greet(peer):
        pl.semaphore_signal(barrier, inc=1, device_id={"flow": peer}, device_id_type=MESH)

    in_turn(greet)
    for step in (1, trans_size - 1):
        pl.semaphore_signal(
            barrier,
            inc=1,
            device_id={"trans": lax.rem(group + step, trans_size)},
            device_id_type=MESH,
        )
    mobile_rows = 2 * CELLS * PLANES

    def load(source, target, rows, half, index):
        return pltpu.make_async_copy(
            source.at[rows, pl.ds(half * LANES, LANES)],
            target.at[half, rows],
            load_sem.at[index],
        )

    field_span = pl.ds(0, CELLS * PLANES)
    mobile_span = pl.ds(0, mobile_rows)
    immobile_span = pl.ds(mobile_rows, mobile_rows)
    first_loads, later_loads = [], []
    for half in range(HALVES):
        first_loads.append(load(strat_hbm, strat, field_span, half, half))
        first_loads.append(load(conc_hbm, conc, mobile_span, half, 2 + half))
        later_loads.append(load(conc_hbm, conc, immobile_span, half, 4 + half))
    table_loads = [
        pltpu.make_async_copy(src, dst, load_sem.at[6 + index])
        for index, (src, dst) in enumerate(
            (
                (por_hbm, por_ref),
                (disp_hbm, disp_ref),
                (trans_hbm, trans_ref),
                (exch_hbm, exch_ref),
                (decay_hbm, decay_ref),
            )
        )
    ]
    for copy in table_loads + first_loads + later_loads:
        copy.start()

    lane = lax.broadcasted_iota(jnp.int32, (8, LANES), 1)

    def lane_table(read):
        table = jnp.full((8, LANES), read(0), f32)
        for stratum in range(1, STRATA):
            table = jnp.where(lane == stratum, read(stratum), table)
        return table

    for copy in table_loads:
        copy.wait()
    trans = lane_table(lambda k: trans_ref[k])
    tables[TABLES.index("u_t")] = 0.5 / trans

    def look(name, picked):
        table = tables[TABLES.index(name)]
        wide = jnp.concatenate([table] * (picked.shape[0] // 8), axis=0)
        return jnp.take_along_axis(wide, picked, axis=1, mode="promise_in_bounds")

    def spot(cell):
        start = cell * PLANES
        if not isinstance(cell, int):
            start = pl.multiple_of(start, PLANES)
        return pl.ds(start, PLANES)

    def strata_of(cell):
        return strat[:, spot(cell), :].reshape(ROWS, LANES)

    def conc_of(component, cell):
        return conc[:, spot(component * CELLS + cell), :].reshape(ROWS, LANES)

    def get(name, cell):
        return fields[FIELDS.index(name), :, spot(cell), :].reshape(ROWS, LANES)

    def put(name, cell, value):
        fields[FIELDS.index(name), :, spot(cell), :] = value.reshape(HALVES, PLANES, LANES)

    for copy in first_loads:
        copy.wait()

    for side, plane in ((0, 0), (1, PLANES - 1)):
        for half in range(HALVES):
            rows = pl.ds(plane, CELLS, stride=PLANES)
            picked = strat[half, rows, :]
            edges[side, half, pl.ds(0, CELLS), :] = look("u_t", picked)
            for component in range(2):
                rows = pl.ds(component * CELLS * PLANES + plane, CELLS, stride=PLANES)
                edges[side, half, pl.ds((component + 1) * CELLS, CELLS), :] = conc[half, rows, :]

    por = lane_table(lambda k: por_ref[k])
    disp_a = lane_table(lambda k: disp_ref[0, k])
    disp_b = lane_table(lambda k: disp_ref[1, k])
    exch = lane_table(lambda k: exch_ref[k])
    decay = lane_table(lambda k: decay_ref[k])
    rest = 1.0 - por
    m_a = 1.0 / (rest + exch + decay)
    m_b = 1.0 / (rest + exch)
    values = {
        "u_a": 0.5 / disp_a,
        "u_b": 0.5 / disp_b,
        "g_a": por + decay + exch * (rest + decay) * m_a,
        "g_b": por + exch * rest * m_b,
        "eta": decay + exch * exch * decay * m_a * m_b,
        "por": por,
        "src_a": exch * rest * m_a,
        "src_b": exch * rest * m_b,
        "src_ab": exch * m_b * decay * rest * m_a,
        "im_a": rest * m_a,
        "ex_a": exch * m_a,
        "im_b": rest * m_b,
        "ex_b": exch * m_b,
        "im_ab": decay * m_b * rest * m_a,
        "ex_ab": decay * m_b * exch * m_a,
    }
    for name, value in values.items():
        tables[TABLES.index(name)] = value

    def eliminate(state, name, r, g_next):
        k, alpha, delta = state
        w = 1.0 / (1.0 + r * (k + delta))
        rw = r * w
        q = rw * k
        return (k * w, alpha + q * delta, g_next + delta * w), w, q, rw

    first = strata_of(0)
    zero = jnp.zeros((ROWS, LANES), f32)
    u_a0, u_b0 = look("u_a", first), look("u_b", first)
    start = (
        (1.0 / u_a0, zero, look("g_a", first)),
        (1.0 / u_b0, zero, look("g_b", first)),
        u_a0,
        u_b0,
    )

    def forward(cell, state, last=False):
        state_a, state_b, u_a, u_b = state
        if last:
            u_a_next, u_b_next, g_a_next, g_b_next = zero, zero, zero, zero
        else:
            picked = strata_of(cell + 1)
            u_a_next, u_b_next = look("u_a", picked), look("u_b", picked)
            g_a_next, g_b_next = look("g_a", picked), look("g_b", picked)
        state_a, w, q, r = eliminate(state_a, "a", u_a + u_a_next, g_a_next)
        put("w_a", cell, w)
        put("q_a", cell, q)
        put("r_a", cell, r)
        state_b, w, q, r = eliminate(state_b, "b", u_b + u_b_next, g_b_next)
        put("w_b", cell, w)
        put("q_b", cell, q)
        put("r_b", cell, r)
        return state_a, state_b, u_a_next, u_b_next

    state = lax.fori_loop(0, CELLS - 1, forward, start, unroll=5)
    relation_a, relation_b, _, _ = forward(CELLS - 1, state, last=True)

    one = jnp.ones((ROWS, LANES), f32)

    def cumulate(step, state):
        q_a, w_a, q_b, w_b, c_ll, c_lr, c_rl, c_rr = state
        cell = CELLS - 1 - step
        eta = look("eta", strata_of(cell))
        put("eta", cell, eta)
        now = get("w_a", cell)
        q_a, w_a = now * q_a + get("q_a", cell), now * w_a
        now = get("w_b", cell)
        q_b, w_b = now * q_b + get("q_b", cell), now * w_b
        put("q_cum_a", cell, q_a)
        put("w_cum_a", cell, w_a)
        put("q_cum_b", cell, q_b)
        put("w_cum_b", cell, w_b)
        eta_q, eta_w = eta * q_a, eta * w_a
        return (
            q_a,
            w_a,
            q_b,
            w_b,
            c_ll + q_b * eta_q,
            c_lr + q_b * eta_w,
            c_rl + w_b * eta_q,
            c_rr + w_b * eta_w,
        )

    state = lax.fori_loop(
        0, CELLS, cumulate, (zero, one, zero, one, zero, zero, zero, zero), unroll=4
    )
    cross = state[4:]
    pl.semaphore_wait(barrier, flow_size + 1)

    def edge_copy(side):
        return pltpu.make_async_remote_copy(
            src_ref=edges.at[side],
            dst_ref=halo.at[1 - side],
            send_sem=edge_send_sem.at[side],
            recv_sem=edge_recv_sem.at[1 - side],
            device_id={"trans": group - 1 + 2 * side},
            device_id_type=MESH,
        )

    has_side = (group > 0, group < trans_size - 1)

    @pl.when(has_side[0])
    def _():
        edge_copy(0).start()

    @pl.when(has_side[1])
    def _():
        edge_copy(1).start()

    k_a, alpha_a, delta_a = relation_a
    k_b, alpha_b, delta_b = relation_b

    def exchange(source, target, send_sem, recv_sem, fan_out):
        def push(peer):
            pltpu.make_async_remote_copy(
                src_ref=source.at[peer],
                dst_ref=target.at[me],
                send_sem=send_sem,
                recv_sem=recv_sem,
                device_id={"flow": peer},
                device_id_type=MESH,
            ).start()

        fan_out(push)
        target[me] = source[me]

    def total_wait(source, target, sem):
        span = pl.ds(0, flow_size - 1)
        pltpu.make_async_copy(source.at[span], target.at[span], sem).wait()

    for index, part in enumerate((k_a, alpha_a, delta_a, k_b, alpha_b, delta_b, *cross)):
        matrix_out[:, index, :] = part
    exchange(matrix_out, matrix_in, matrix_send_sem, matrix_recv_sem, in_turn)

    row = lax.broadcasted_iota(jnp.int32, (ROWS, LANES), 0)
    column = lax.broadcasted_iota(jnp.int32, (ROWS, LANES), 1)
    z_last = column == LANES - 1
    z_open = z_last & (row >= PLANES)
    z_first = column == 0

    def swap(x):
        return jnp.concatenate([x[PLANES:], x[:PLANES]], axis=0)

    def next_z(x):
        moved = pltpu.roll(x, LANES - 1, axis=1)
        return jnp.where(z_last, swap(moved), moved)

    def previous_z(x):
        moved = pltpu.roll(x, 1, axis=1)
        return jnp.where(z_first, swap(moved), moved)

    def across(start):
        return pl.ds(start, CELLS, stride=PLANES)

    def strata_plane(plane):
        return jnp.concatenate([strat[half, across(plane), :] for half in range(HALVES)], axis=0)

    def conc_plane(component, plane):
        rows = across(component * CELLS * PLANES + plane)
        return jnp.concatenate([conc[half, rows, :] for half in range(HALVES)], axis=0)

    def put_plane(name, plane, value):
        for half in range(HALVES):
            piece = value[half * CELLS : (half + 1) * CELLS]
            fields[FIELDS.index(name), half, across(plane), :] = piece

    def sources(plane, state):
        picked, u_t, mobile, arriving = state
        ahead = plane + 1 - (plane + 1) // PLANES
        picked_ahead = strata_plane(ahead)
        u_ahead = look("u_t", picked_ahead)
        mobile_ahead = [conc_plane(component, ahead) for component in range(2)]
        h_y = 1.0 / (u_t + u_ahead)
        h_z = jnp.where(z_open, 0.0, 1.0 / (u_t + next_z(u_t)))
        por = look("por", picked)
        leaving, filled = [], []
        for component in range(2):
            x = mobile[component]
            flow_y = h_y * (mobile_ahead[component] - x)
            flow_z = h_z * (next_z(x) - x)
            flux = (flow_y - arriving[component]) + (flow_z - previous_z(flow_z))
            leaving.append(flow_y)
            filled.append(por * x + flux)
        immobile_a, immobile_b = conc_plane(2, plane), conc_plane(3, plane)
        put_plane("s_a", plane, filled[0] + look("src_a", picked) * immobile_a)
        put_plane(
            "s_b",
            plane,
            filled[1] + look("src_b", picked) * immobile_b + look("src_ab", picked) * immobile_a,
        )
        return picked_ahead, u_ahead, mobile_ahead, leaving

    for copy in later_loads:
        copy.wait()
    picked = strata_plane(0)
    start = (
        picked,
        look("u_t", picked),
        [conc_plane(component, 0) for component in range(2)],
        [zero, zero],
    )
    lax.fori_loop(0, PLANES, sources, start, unroll=4)

    def source_forward(cell, state):
        j, j_left = state
        put("v_a", cell, get("r_a", cell) * j)
        j_left = j_left + get("q_a", cell) * j
        return get("s_a", cell + 1) + get("w_a", cell) * j, j_left

    last_cell = CELLS - 1

    def totals(keep):
        j, j_left = lax.fori_loop(
            0, last_cell, source_forward, (get("s_a", 0), zero), unroll=5
        )
        put("v_a", last_cell, get("r_a", last_cell) * j)
        j_left_a = j_left + get("q_a", last_cell) * j
        j_right_a = get("w_a", last_cell) * j

        def source_backward(step, state):
            p, j_left, j_right = state
            cell = CELLS - 1 - step
            p = get("w_a", cell) * p + get("v_a", cell)
            forcing = get("s_b", cell) + get("eta", cell) * p
            if keep:
                put("v_a", cell, p)
                put("s_b", cell, forcing)
            j_left = j_left + get("q_cum_b", cell) * forcing
            return p, j_left, j_right + get("w_cum_b", cell) * forcing

        _, j_left_b, j_right_b = lax.fori_loop(
            0, CELLS, source_backward, (zero, zero, zero), unroll=4
        )
        return j_left_a, j_right_a, j_left_b, j_right_b

    def post(source, peer):
        pltpu.make_async_remote_copy(
            src_ref=source,
            dst_ref=source_in.at[me],
            send_sem=source_send_sem,
            recv_sem=source_recv_sem,
            device_id={"flow": peer},
            device_id_type=MESH,
        ).start()

    def is_inner(peer):
        place_in_half = lax.rem(peer, PLANES)
        return (place_in_half > 0) & (place_in_half < PLANES - 1)

    for index, part in enumerate(totals(keep=False)):
        source_out[:, index, :] = part

    def post_inner(peer):
        @pl.when(is_inner(peer))
        def _():
            post(source_out.at[peer], peer)

    in_turn(post_inner)

    @pl.when(is_inner(me))
    def _():
        source_in[me] = source_out[me]

    def edge_wait(side):
        pltpu.make_async_copy(
            edges.at[side], halo.at[side], edge_recv_sem.at[side]
        ).wait()

    for side in range(2):

        @pl.when(has_side[side])
        def _(side=side):
            edge_wait(side)
            rows = pl.ds(side * (PLANES - 1), CELLS, stride=PLANES)
            for half in range(HALVES):
                own = [edges[side, half, pl.ds(k * CELLS, CELLS), :] for k in range(3)]
                other = [halo[side, half, pl.ds(k * CELLS, CELLS), :] for k in range(3)]
                h = 1.0 / (own[0] + other[0])
                for component, name in ((1, "s_a"), (2, "s_b")):
                    spot_in = (FIELDS.index(name), half, rows, slice(None))
                    fields[spot_in] = fields[spot_in] + h * (other[component] - own[component])

    for index, part in enumerate(totals(keep=True)):
        for position, edge_row in enumerate(EDGE_ROWS):
            edge_out[position, index : index + 1, :] = part[edge_row : edge_row + 1]
    for position, edge_row in enumerate(EDGE_ROWS):

        @pl.when(me != edge_row)
        def _(position=position, edge_row=edge_row):
            post(edge_out.at[position], edge_row)

    for position, edge_row in enumerate(EDGE_ROWS):

        @pl.when(me == edge_row)
        def _(position=position):
            source_in[me] = edge_out[position]

    def basis_forward(cell, state):
        j_0, j_l, j_r = state
        r, w = get("r_b", cell), get("w_b", cell)
        eta = get("eta", cell)
        j_0 = j_0 + get("s_b", cell)
        j_l = j_l + eta * get("q_cum_a", cell)
        j_r = j_r + eta * get("w_cum_a", cell)
        put("p_b", cell, r * j_0)
        put("y_l", cell, r * j_l)
        put("y_r", cell, r * j_r)
        return w * j_0, w * j_l, w * j_r

    lax.fori_loop(0, CELLS, basis_forward, (zero, zero, zero), unroll=4)

    def basis_backward(step, state):
        p, y_l, y_r = state
        cell = CELLS - 1 - step
        w = get("w_b", cell)
        p = w * p + get("p_b", cell)
        y_l = w * y_l + get("y_l", cell)
        y_r = w * y_r + get("y_r", cell)
        put("p_b", cell, p)
        put("y_l", cell, y_l)
        put("y_r", cell, y_r)
        picked = strata_of(cell)
        immobile_a, immobile_b = conc_of(2, cell), conc_of(3, cell)
        put("im_a", cell, look("im_a", picked) * immobile_a)
        put("ex_a", cell, look("ex_a", picked))
        put("im_b", cell, look("im_b", picked) * immobile_b + look("im_ab", picked) * immobile_a)
        put("ex_b", cell, look("ex_b", picked))
        put("ex_ab", cell, look("ex_ab", picked))
        return p, y_l, y_r

    lax.fori_loop(0, CELLS, basis_backward, (zero, zero, zero), unroll=4)

    total_wait(matrix_out, matrix_in, matrix_recv_sem)
    (
        k_a,
        alpha_a,
        delta_a,
        k_b,
        alpha_b,
        delta_b,
        c_ll,
        c_lr,
        c_rl,
        c_rr,
    ) = [matrix_in[:, index, :] for index in range(MATRIX)]
    at_end = row == 0

    def up(x, shift):
        if shift % 8 == 0:
            return jnp.concatenate([x[shift:], x[:shift]], axis=0)
        return pltpu.roll(x, ROWS - shift, axis=0)

    def down(x, shift):
        if shift % 8 == 0:
            return jnp.concatenate([x[ROWS - shift :], x[: ROWS - shift]], axis=0)
        return pltpu.roll(x, shift, axis=0)

    def reduce_matrix(k, alpha, delta):
        h = 1.0 / (k + alpha)
        pull = k * h
        delta = delta + up(jnp.where(at_end, 0.0, alpha), 1)
        delta = delta + jnp.where(at_end, alpha * pull, 0.0)
        coupling = jnp.where(at_end, 0.0, k)
        levels = []
        shift = 1
        while shift < ROWS:
            ahead = up(coupling, shift)
            inverse = 1.0 / (coupling + ahead + delta)
            levels.append((shift, coupling, ahead, inverse))
            shed = delta * inverse
            delta = delta + coupling * down(shed, shift) + ahead * up(shed, shift)
            coupling = coupling * down(coupling * inverse, shift)
            shift *= 2
        return h, pull, levels, 1.0 / delta

    def reduce_source(reduced, k, j_left, j_right):
        h, pull, levels, inverse_delta = reduced
        j = j_right + up(jnp.where(at_end, 0.0, j_left), 1)
        j = j + jnp.where(at_end, pull * j_left, 0.0)
        for shift, coupling, ahead, inverse in levels:
            shed = j * inverse
            j = j + coupling * down(shed, shift) + ahead * up(shed, shift)
        right = j * inverse_delta
        left = jnp.where(at_end, h * (j_left + k * right), down(right, 1))
        return left, right

    reduced_a = reduce_matrix(k_a, alpha_a, delta_a)
    reduced_b = reduce_matrix(k_b, alpha_b, delta_b)
    total_wait(source_out, source_in, source_recv_sem)
    j_left_a, j_right_a, j_left_b, j_right_b = [
        source_in[:, index, :] for index in range(SOURCE)
    ]
    left_a, right_a = reduce_source(reduced_a, k_a, j_left_a, j_right_a)
    left_b, right_b = reduce_source(
        reduced_b,
        k_b,
        j_left_b + c_ll * left_a + c_lr * right_a,
        j_right_b + c_rl * left_a + c_rr * right_a,
    )
    for index, part in enumerate((left_a, right_a, left_b, right_b)):
        back[:, index, :] = part
    exchange(back, got, back_send_sem, back_recv_sem, in_turn)
    total_wait(back, got, back_recv_sem)
    for index in range(SOURCE):
        ends[index] = got[:, index, :]

    for side in range(2):

        @pl.when(has_side[side])
        def _(side=side):
            edge_copy(side).wait_send()

    total_wait(matrix_out, matrix_in, matrix_send_sem)
    total_wait(source_out, source_in, source_send_sem)
    total_wait(back, got, back_send_sem)


def spread(start, size):
    return pl.ds(pl.multiple_of(start, PLANES), size)


def finish(fields, ends, out_hbm, out, out_sem):
    left_a, right_a, left_b, right_b = [ends[index] for index in range(SOURCE)]

    def get(name, cell):
        rows = spread(cell * PLANES, PLANES)
        return fields[FIELDS.index(name), :, rows, :].reshape(ROWS, LANES)

    def store(component, cell, value):
        rows = spread((component * CELLS + cell) * PLANES, PLANES)
        for half in range(HALVES):
            piece = value[half * PLANES : (half + 1) * PLANES]
            out[rows, pl.ds(half * LANES, LANES)] = piece

    def leave(chunk, component):
        rows = spread((component * CELLS + chunk * CHUNK) * PLANES, CHUNK * PLANES)
        return pltpu.make_async_copy(
            out.at[rows], out_hbm.at[rows], out_sem.at[chunk * 4 + component]
        )

    def fill(chunk, carry):
        for step in range(CHUNK):
            cell = chunk * CHUNK + step
            a = get("v_a", cell) + get("q_cum_a", cell) * left_a + get("w_cum_a", cell) * right_a
            b = (
                get("p_b", cell)
                + get("q_cum_b", cell) * left_b
                + get("w_cum_b", cell) * right_b
                + get("y_l", cell) * left_a
                + get("y_r", cell) * right_a
            )
            store(0, cell, a)
            store(1, cell, b)
            store(2, cell, get("im_a", cell) + get("ex_a", cell) * a)
            store(3, cell, get("im_b", cell) + get("ex_b", cell) * b + get("ex_ab", cell) * a)
        for component in range(4):
            leave(chunk, component).start()
        return carry

    def settle(chunk, carry):
        for component in range(4):
            leave(chunk, component).wait()
        return carry

    lax.fori_loop(0, CELLS // CHUNK, fill, 0)
    lax.fori_loop(0, CELLS // CHUNK, settle, 0)


def per_device(
    flow_size,
    trans_size,
    concentration,
    stratum,
    porosity,
    dispersion_table,
    transverse_table,
    exchange_table,
    decay_table,
):
    f32 = jnp.float32
    components, cells, planes, width = concentration.shape
    total = components * cells * planes
    field_rows = cells * planes
    hbm = pl.BlockSpec(memory_space=pltpu.HBM)
    vmem = pl.BlockSpec(memory_space=pltpu.VMEM)
    fields, ends = pl.pallas_call(
        functools.partial(kernel, flow_size, trans_size),
        out_shape=(
            jax.ShapeDtypeStruct((len(FIELDS), HALVES, field_rows, LANES), f32),
            jax.ShapeDtypeStruct((SOURCE, ROWS, LANES), f32),
        ),
        in_specs=[hbm] * 7,
        out_specs=(vmem, vmem),
        scratch_shapes=[
            pltpu.SMEM((STRATA,), f32),
            pltpu.SMEM((2, STRATA), f32),
            pltpu.SMEM((STRATA,), f32),
            pltpu.SMEM((STRATA,), f32),
            pltpu.SMEM((STRATA,), f32),
            pltpu.VMEM((HALVES, total, LANES), f32),
            pltpu.VMEM((HALVES, field_rows, LANES), jnp.int32),
            pltpu.VMEM((len(TABLES), 8, LANES), f32),
            pltpu.VMEM((2, HALVES, 3 * CELLS, LANES), f32),
            pltpu.VMEM((2, HALVES, 3 * CELLS, LANES), f32),
            pltpu.VMEM((flow_size, MATRIX, LANES), f32),
            pltpu.VMEM((flow_size, MATRIX, LANES), f32),
            pltpu.VMEM((flow_size, SOURCE, LANES), f32),
            pltpu.VMEM((len(EDGE_ROWS), SOURCE, LANES), f32),
            pltpu.VMEM((flow_size, SOURCE, LANES), f32),
            pltpu.VMEM((flow_size, SOURCE, LANES), f32),
            pltpu.VMEM((flow_size, SOURCE, LANES), f32),
            pltpu.SemaphoreType.DMA((11,)),
            pltpu.SemaphoreType.DMA((2,)),
            pltpu.SemaphoreType.DMA((2,)),
            pltpu.SemaphoreType.DMA,
            pltpu.SemaphoreType.DMA,
            pltpu.SemaphoreType.DMA,
            pltpu.SemaphoreType.DMA,
            pltpu.SemaphoreType.DMA,
            pltpu.SemaphoreType.DMA,
        ],
        compiler_params=pltpu.CompilerParams(
            collective_id=0, has_side_effects=True, vmem_limit_bytes=32 * 1024 * 1024
        ),
    )(
        *(
            pltpu.with_memory_space_constraint(x, pltpu.HBM)
            for x in (
                concentration.reshape(total, width),
                stratum.reshape(field_rows, width),
                porosity,
                dispersion_table.T,
                transverse_table,
                exchange_table,
                decay_table,
            )
        )
    )
    solved = pl.pallas_call(
        finish,
        out_shape=jax.ShapeDtypeStruct((total, width), f32),
        in_specs=[vmem, vmem],
        out_specs=hbm,
        scratch_shapes=[
            pltpu.VMEM((total, width), f32),
            pltpu.SemaphoreType.DMA((4 * CELLS // CHUNK,)),
        ],
        compiler_params=pltpu.CompilerParams(vmem_limit_bytes=16 * 1024 * 1024),
    )(
        pltpu.with_memory_space_constraint(fields, pltpu.VMEM),
        pltpu.with_memory_space_constraint(ends, pltpu.VMEM),
    )
    return solved.reshape(concentration.shape)


def solution(mesh):
    in_specs = (P(None, "flow", "trans", None), P("flow", "trans", None), P(), P(), P(), P(), P())
    out_specs = P(None, "flow", "trans", None)
    return jax.shard_map(
        functools.partial(per_device, mesh.shape["flow"], mesh.shape["trans"]),
        mesh=mesh,
        in_specs=in_specs,
        out_specs=out_specs,
        check_vma=False,
    )
```
